128 devices in a mesh: clus: 16 (over x, z), tgt: 8 (over y, core).
Axes of the slice: x: 4, y: 4, z: 4, core: 2. Of those that a mesh axis runs over, the one named last changes fastest.
Arguments:
- src_pos: float32 [3, 262144], P(None, ('clus', 'tgt')), may hold values from 0 to 1
- src_weight: float32 [262144], P(('clus', 'tgt')), may hold values from 0.1 to 1
- src_pot: float32 [262144], P(('clus', 'tgt')), may hold values from -0.1 to 0.05
- src_count: int32 [1024], P(('clus', 'tgt')), may hold values from 128 to 256, as said below
- tgt_pos: float32 [3, 262144], P(None, ('clus', 'tgt')), may hold values from 0 to 1
- tgt_weight: float32 [262144], P(('clus', 'tgt')), may hold values from 0.1 to 1
- tgt_pot: float32 [262144], P(('clus', 'tgt')), may hold values from -0.1 to 0.05
- tgt_count: int32 [1024], P(('clus', 'tgt')), may hold values from 128 to 256, as said below
- requests: int32 [2048, 2], P(('clus', 'tgt')), may hold values from 0 to 7, as said below
- pair_src: int32 [8192], P(('clus', 'tgt')), may hold values from 0 to 63, as said below
- pair_slot: int32 [8192], P(('clus', 'tgt')), may hold values from 0 to 31, as said below
- pair_count: int32 [128], P(('clus', 'tgt')), may hold values from 32 to 64, as said below
Outputs:
- grad_src_pos: float32 [3, 262144], P(None, ('clus', 'tgt'))
- grad_src_weight: float32 [262144], P(('clus', 'tgt'))
- grad_tgt_pos: float32 [3, 262144], P(None, ('clus', 'tgt'))
- grad_tgt_weight: float32 [262144], P(('clus', 'tgt'))
The draws below stay inside these ranges and needn't reach their ends.
Inputs may be any that keep to these rules, and one draw needn't show every extreme that they name: `src_count`: counts of live points, the rest of each block is padding; some block is full and some is half full. `tgt_count`: counts of live points, the rest of each block is padding; some block is full and some is half full. `requests`: each row holds 2 different local block numbers of one owner: row r of group d names blocks of the owner with clus index r and the tgt index of d. `pair_src`: source block within the group's 64 source blocks of its clus index, all tgt indices in order. `pair_slot`: slot r * 2 + m of the group's request rows; the live entries of a group name every one of its 32 slots. `pair_count`: entries past the count are padding with valid numbers and must not count.
All inputs are finite; a program needn't handle non-finite values.
Results may differ from the reference program's by a relative error of at most 0.0003.
Values sent between devices are 32-bit elements; how exact they have to be, the bound alone decides.
A program may use at most 64 MiB of HBM per device.

```python
import math
import jax
import jax.numpy as jnp
from jax import lax

BLK = 256
TB_DEV = 8
REQ = 2
DEV_COUNT = 128
SB_GROUP = 64
SLOTS = 32
PAIRS_DEV = 64
NSB = 1024
NTB = 1024
NS = 262144
NT = 262144
N_CLUS = 16
N_TGT = 8


def block_counts(key, total):
    counts = jax.random.randint(key, (total,), BLK // 2, BLK + 1, dtype=jnp.int32)
    return counts.at[0].set(BLK).at[1].set(BLK // 2)


def draw_src_count(key, part):
    return block_counts(jax.random.fold_in(key, 11), NSB)


def draw_tgt_count(key, part):
    return block_counts(jax.random.fold_in(key, 12), NTB)


def pick_row(row_key):
    return jax.random.permutation(row_key, TB_DEV)[:REQ].astype(jnp.int32)


def draw_requests(key, part):
    row_keys = jax.random.split(jax.random.fold_in(key, 13), DEV_COUNT * N_CLUS)
    picks = jax.vmap(pick_row)(row_keys)
    spread = jnp.arange(REQ, dtype=jnp.int32) * (TB_DEV - 1) // (REQ - 1)
    return picks.at[0].set(spread)


def slot_perm(row_key):
    return jax.random.permutation(row_key, SLOTS).astype(jnp.int32)


def pair_table(key):
    base = jax.random.fold_in(key, 17)
    first_key, step_key, slot_key, order_key = jax.random.split(base, 4)
    first = jax.random.randint(first_key, (DEV_COUNT, SLOTS), 0, SB_GROUP, dtype=jnp.int32)
    first = first.at[0, 0].set(0).at[0, 1].set(SB_GROUP - 1)
    offset = jax.random.randint(step_key, (DEV_COUNT, SLOTS), 1, SB_GROUP, dtype=jnp.int32)
    second = (first + offset) % SB_GROUP
    slot_order = jax.vmap(slot_perm)(jax.random.split(slot_key, DEV_COUNT))
    shuffle = jax.vmap(slot_perm)(jax.random.split(order_key, DEV_COUNT))
    second_src = jnp.take_along_axis(second, shuffle, 1)
    second_slot = jnp.take_along_axis(slot_order, shuffle, 1)
    sources = jnp.concatenate([first, second_src], 1).reshape(-1)
    slots = jnp.concatenate([slot_order, second_slot], 1).reshape(-1)
    return (sources.astype(jnp.int32), slots.astype(jnp.int32))


def draw_pair_src(key, part):
    return pair_table(key)[0]


def draw_pair_slot(key, part):
    return pair_table(key)[1]


def draw_pair_count(key, part):
    counts = jax.random.randint(jax.random.fold_in(key, 19), (DEV_COUNT,), SLOTS, PAIRS_DEV + 1, dtype=jnp.int32)
    return counts.at[0].set(PAIRS_DEV).at[1].set(SLOTS)


def levels(key, extent, cuts, smallest, top_value):
    def one(dim, shards_of):
        steps = jax.random.uniform(jax.random.fold_in(jax.random.fold_in(key, 6), dim), (shards_of,), jnp.float32, smallest / len(cuts), top_value / len(cuts))
        return jnp.repeat(jnp.exp(steps), extent[dim] // shards_of).reshape((-1,) + (1,) * (len(extent) - dim - 1))

    gain = one(*cuts[0])
    for cut in cuts[1:]:
        gain = gain * one(*cut)
    return gain


def setup_inputs(seed: int = 0) -> dict:
    streams_of = jax.random.split(jax.random.key(seed), 13)
    return {
        "src_pos": jnp.clip(1.0 * jax.random.uniform(streams_of[0], (3, NS), jnp.float32) ** levels(streams_of[0], (3, NS), ((1, 128),), -0.2, 0.2), 0.0, 1.0),
        "src_weight": jnp.clip(jnp.exp(math.log(1.0) - 2.3025851 * jax.random.uniform(streams_of[1], (NS,), jnp.float32) ** levels(streams_of[1], (NS,), ((0, 128),), -0.2, 0.2)), 0.1, 1.0),
        "src_pot": jnp.clip(-0.1 + 0.15 * jax.random.uniform(streams_of[2], (NS,), jnp.float32) ** levels(streams_of[2], (NS,), ((0, 128),), -0.2, 0.2), -0.1, 0.05),
        "src_count": draw_src_count(jax.random.fold_in(streams_of[12], 71), 0),
        "tgt_pos": jnp.clip(1.0 * jax.random.uniform(streams_of[4], (3, NT), jnp.float32) ** levels(streams_of[4], (3, NT), ((1, 128),), -0.2, 0.2), 0.0, 1.0),
        "tgt_weight": jnp.clip(jnp.exp(math.log(1.0) - 2.3025851 * jax.random.uniform(streams_of[5], (NT,), jnp.float32) ** levels(streams_of[5], (NT,), ((0, 128),), -0.2, 0.2)), 0.1, 1.0),
        "tgt_pot": jnp.clip(-0.1 + 0.15 * jax.random.uniform(streams_of[6], (NT,), jnp.float32) ** levels(streams_of[6], (NT,), ((0, 128),), -0.2, 0.2), -0.1, 0.05),
        "tgt_count": draw_tgt_count(jax.random.fold_in(streams_of[12], 71), 0),
        "requests": draw_requests(jax.random.fold_in(streams_of[12], 71), 0),
        "pair_src": draw_pair_src(jax.random.fold_in(streams_of[12], 71), 0),
        "pair_slot": draw_pair_slot(jax.random.fold_in(streams_of[12], 71), 0),
        "pair_count": draw_pair_count(jax.random.fold_in(streams_of[12], 71), 0),
    }


entropic = 0.05
highest = lax.Precision.HIGHEST


def local_pack(positions, weights, potentials, counts):
    block_count = counts.shape[0]
    block_len = positions.shape[1] // block_count
    offsets = jnp.arange(block_len, dtype=jnp.int32)[None, :]
    live_mask = (offsets < counts[:, None]).astype(jnp.float32).reshape(-1)
    packed = jnp.concatenate([positions, (weights * live_mask)[None, :], potentials[None, :]], 0)
    return packed, live_mask


def tile_kernel(src_tiles, tgt_tiles, live_mask):
    crossed = jnp.einsum("cpi,cpj->pij", src_tiles[:3], tgt_tiles[:3], precision=highest)
    left_part = src_tiles[4] - 0.5 * jnp.sum(src_tiles[:3] * src_tiles[:3], 0)
    right_part = tgt_tiles[4] - 0.5 * jnp.sum(tgt_tiles[:3] * tgt_tiles[:3], 0)
    expo = (left_part[:, :, None] + right_part[:, None, :] + crossed) / entropic
    return jnp.exp(expo) * live_mask[:, None, None]


def source_terms(kernel, src_tiles, tgt_tiles):
    weighted = kernel * tgt_tiles[3][:, None, :]
    row_totals = jnp.sum(weighted, 2)
    shifted = jnp.einsum("pij,cpj->cpi", weighted, tgt_tiles[:3], precision=highest)
    motion = src_tiles[3][None] * (src_tiles[:3] * row_totals[None] - shifted)
    return jnp.concatenate([motion, (-entropic * row_totals)[None]], 0)


def target_terms(kernel, src_tiles, tgt_tiles):
    weighted = kernel * src_tiles[3][:, :, None]
    col_totals = jnp.sum(weighted, 1)
    shifted = jnp.einsum("pij,cpi->cpj", weighted, src_tiles[:3], precision=highest)
    motion = tgt_tiles[3][None] * (tgt_tiles[:3] * col_totals[None] - shifted)
    return jnp.concatenate([motion, (-entropic * col_totals)[None]], 0)


def reference(src_pos, src_weight, src_pot, src_count, tgt_pos, tgt_weight, tgt_pot, tgt_count, requests, pair_src, pair_slot, pair_count):
    src_packed, src_live = local_pack(src_pos, src_weight, src_pot, src_count)
    tgt_packed, tgt_live = local_pack(tgt_pos, tgt_weight, tgt_pot, tgt_count)
    src_blocks = src_packed.reshape(5, NSB, BLK)
    tgt_blocks = tgt_packed.reshape(5, NTB, BLK)
    device_ids = jnp.arange(DEV_COUNT, dtype=jnp.int32)
    slabs = requests.reshape(DEV_COUNT, N_CLUS, REQ)

    def one_device(carry, inputs):
        src_acc, tgt_acc = carry
        device, sources, slots, live_pairs, slab = inputs
        clus_idx = device // N_TGT
        tgt_idx = device % N_TGT
        src_index = (clus_idx * SB_GROUP + sources).astype(jnp.int32)
        peers = slots // REQ
        ranks = slots % REQ
        tgt_index = ((peers * N_TGT + tgt_idx) * TB_DEV + slab[peers, ranks]).astype(jnp.int32)
        live_mask = (jnp.arange(PAIRS_DEV, dtype=jnp.int32) < live_pairs).astype(jnp.float32)
        src_tiles = jnp.take(src_blocks, src_index, axis=1)
        tgt_tiles = jnp.take(tgt_blocks, tgt_index, axis=1)
        kernel = tile_kernel(src_tiles, tgt_tiles, live_mask)
        src_acc = src_acc.at[:, src_index, :].add(source_terms(kernel, src_tiles, tgt_tiles))
        tgt_acc = tgt_acc.at[:, tgt_index, :].add(target_terms(kernel, src_tiles, tgt_tiles))
        return (src_acc, tgt_acc), None

    start = (jnp.zeros((4, NSB, BLK), jnp.float32), jnp.zeros((4, NTB, BLK), jnp.float32))
    scanned = (device_ids, pair_src.reshape(DEV_COUNT, PAIRS_DEV), pair_slot.reshape(DEV_COUNT, PAIRS_DEV), pair_count, slabs)
    (src_acc, tgt_acc), _ = lax.scan(one_device, start, scanned)
    src_sums = src_acc.reshape(4, NS)
    tgt_sums = tgt_acc.reshape(4, NT)
    grad_src_pos = src_sums[:3] * src_live[None, :]
    grad_src_weight = (src_pot + src_sums[3]) * src_live
    grad_tgt_pos = tgt_sums[:3] * tgt_live[None, :]
    grad_tgt_weight = (tgt_pot + tgt_sums[3]) * tgt_live
    return grad_src_pos, grad_src_weight, grad_tgt_pos, grad_tgt_weight
```

```python
import functools
import math

import jax
import jax.numpy as jnp
from jax import lax
from jax.experimental import pallas as pl
from jax.experimental.pallas import tpu as pltpu
from jax.sharding import Mesh
from jax.sharding import PartitionSpec as P

AXES = ("x", "z", "y", "core")
MESH = pl.DeviceIdType.MESH
BLK = 256
LANES = 128
OWN = 8
REQ = 2
ENTROPIC = 0.05
SCALE = 1.0 / (ENTROPIC * math.log(2.0))
DEAD = -1.0e4
f32 = jnp.float32
bf16 = jnp.bfloat16


def split3(v):
    hi = v.astype(bf16).astype(f32)
    rest = v - hi
    mid = rest.astype(bf16).astype(f32)
    return hi, mid, rest - mid


def rows_of(shape):
    return lax.broadcasted_iota(jnp.int32, shape, 0)


def pack(pos_ref, weight_ref, pot_ref, count_ref):
    quarters = weight_ref.shape[0]
    row = rows_of((quarters, LANES))
    lane = lax.broadcasted_iota(jnp.int32, (quarters, LANES), 1)
    counts = jnp.zeros((quarters, LANES), jnp.int32)
    for b in range(OWN):
        counts = jnp.where((row >> 1) == b, count_ref[b], counts)
    live = ((row & 1) * LANES + lane) < counts
    xs = [pos_ref[c] - 0.5 for c in range(3)]
    square = xs[0] * xs[0] + xs[1] * xs[1] + xs[2] * xs[2]
    level = SCALE * (pot_ref[...] - 0.5 * square) + jnp.log(weight_ref[...]) * (1.0 / math.log(2.0))
    return xs, jnp.where(live, level, DEAD), live


def put_tiles(tiles, comps):
    for c, comp in enumerate(comps):
        tiles[pl.ds(c, 2 * OWN, stride=4), :] = comp


def get_tiles(tiles):
    return [tiles[pl.ds(c, 2 * OWN, stride=4), :] for c in range(4)]


def unfold(tile):
    return jnp.concatenate([tile, pltpu.roll(tile, 4, 0)], axis=1)


def sum_weights(v, row):
    w = jnp.where((row & 3) == 3, 1.0, v)
    hi = w.astype(bf16).astype(f32)
    return jnp.concatenate([hi, w - hi], axis=0).astype(bf16)


def kernel(
    dims,
    pair_src,
    pair_slot,
    pair_count,
    requests,
    src_count,
    tgt_count,
    src_row,
    slot_row,
    src_pos,
    src_weight,
    src_pot,
    tgt_pos,
    tgt_weight,
    tgt_pot,
    out_src_pos,
    out_src_weight,
    out_tgt_pos,
    out_tgt_weight,
    src_all,
    row_all,
    tgt_all,
    chosen,
    own_req,
    z_req,
    back_req,
    xx,
    yy,
    src_w,
    tgt_w,
    src_parts,
    tgt_parts,
    src_send,
    tgt_send,
    src_back,
    tgt_back,
    total,
    x_send,
    x_recv,
    q_send,
    q_recv,
    s_send,
    s_recv,
    z_send,
    z_recv,
    b_send,
    b_recv,
    t_send,
    t_recv,
    r_send,
    r_recv,
):
    nx, nz, ny, nc = dims
    n_tgt, n_clus = ny * nc, nx * nz
    slots = n_clus * REQ
    pairs = pair_src.shape[0]
    mx, mz, my, mc = (lax.axis_index(a) for a in AXES)
    mt, mr = my * nc + mc, mx * nz + mz

    def at_x(d):
        return lax.rem(mx + d, nx)

    def at_z(d):
        return lax.rem(mz + d, nz)

    def at_t(d):
        return lax.rem(mt + d, n_tgt)

    def at_r(d):
        return lax.rem(mr + d, n_clus)

    def in_tgt(t):
        return (mx, mz, t // nc, lax.rem(t, nc))

    def in_clus(r):
        return (r // nz, lax.rem(r, nz), my, mc)

    def send(src, dst, send_sem, recv_sem, device):
        return pltpu.make_async_remote_copy(
            src_ref=src,
            dst_ref=dst,
            send_sem=send_sem,
            recv_sem=recv_sem,
            device_id=device,
            device_id_type=MESH,
        )

    barrier = pltpu.get_barrier_semaphore()
    for d in range(1, nx):
        pl.semaphore_signal(barrier, inc=1, device_id=(at_x(d), mz, my, mc), device_id_type=MESH)
    for d in range(1, nz):
        pl.semaphore_signal(barrier, inc=1, device_id=(mx, at_z(d), my, mc), device_id_type=MESH)
    for d in range(1, n_tgt):
        pl.semaphore_signal(barrier, inc=1, device_id=in_tgt(at_t(d)), device_id_type=MESH)

    txs, tlevel, tlive = pack(tgt_pos, tgt_weight, tgt_pot, tgt_count)
    put_tiles(row_all.at[mx], txs + [tlevel])
    sxs, slevel, slive = pack(src_pos, src_weight, src_pot, src_count)
    put_tiles(src_all.at[mt], sxs + [slevel])
    for r in range(n_clus):
        for m in range(REQ):
            own_req[r % nz, r // nz, m] = jnp.full((LANES,), requests[r, m], jnp.int32)

    pl.semaphore_wait(barrier, nx - 1 + nz - 1 + n_tgt - 1)

    x_copies = [
        send(row_all.at[mx], row_all.at[mx], x_send.at[d], x_recv.at[d], (at_x(d), mz, my, mc))
        for d in range(1, nx)
    ]
    q_copies = [
        send(own_req.at[at_z(d)], z_req.at[mz], q_send.at[d], q_recv.at[d], (mx, at_z(d), my, mc))
        for d in range(1, nz)
    ]
    s_copies = [
        send(src_all.at[mt], src_all.at[mt], s_send.at[d], s_recv.at[d], in_tgt(at_t(d)))
        for d in range(1, n_tgt)
    ]
    for copy in x_copies + q_copies + s_copies:
        copy.start()
    z_req[mz] = own_req[mz]

    for copy in q_copies + x_copies:
        copy.wait_recv()

    def choose(asked, put):
        for x in range(nx):
            blocks = [row_all[x, b * 8 : b * 8 + 8, :] for b in range(OWN)]
            for m in range(REQ):
                which = jnp.broadcast_to(z_req[asked, x, m : m + 1, :], (8, LANES))
                tile = blocks[0]
                for b in range(1, OWN):
                    tile = jnp.where(which == b, blocks[b], tile)
                put(x, m, tile)

    z_copies = []
    for d in range(1, nz):

        def put(x, m, tile, d=d):
            chosen[d, x, m] = tile

        choose(at_z(d), put)
        copy = send(
            chosen.at[d], tgt_all.at[mz], z_send.at[d], z_recv.at[d], (mx, at_z(d), my, mc)
        )
        copy.start()
        z_copies.append(copy)

    def put_own(x, m, tile):
        tgt_all[mz, x, m] = tile

    choose(mz, put_own)

    row8 = rows_of((8, BLK))
    ones3 = jnp.where(row8 < 3, 1.0, 0.0)
    zeros = jnp.zeros((8, BLK), f32)

    for copy in s_copies:
        copy.wait_recv()

    def prepare_src(i, carry):
        v = unfold(src_all[i // OWN, pl.ds(pl.multiple_of(lax.rem(i, OWN) * 8, 8), 8), :])
        hi, mid, lo = split3(v)
        xx[i] = jnp.concatenate([hi, mid, hi, lo, hi, mid, ones3, zeros], axis=0).astype(bf16)
        src_w[i] = sum_weights(v, row8)
        return carry

    lax.fori_loop(0, n_tgt * OWN, prepare_src, 0, unroll=2)

    for copy in z_copies:
        copy.wait_recv()

    b_copies = [
        send(
            own_req.at[lax.rem(at_r(d), nz), at_r(d) // nz],
            back_req.at[mr],
            b_send.at[d],
            b_recv.at[d],
            in_clus(at_r(d)),
        )
        for d in range(1, n_clus)
    ]
    for copy in b_copies:
        copy.start()
    back_req[mr] = own_req[mz, mx]

    def prepare_tgt(i, carry):
        r, m = i // REQ, lax.rem(i, REQ)
        v = unfold(tgt_all[lax.rem(r, nz), r // nz, m])
        hi, mid, lo = split3(jnp.where(row8 < 3, SCALE * v, jnp.where(row8 == 3, 1.0, 0.0)))
        lhi, lmid, llo = split3(jnp.broadcast_to(v[3:4, :], (8, BLK)))
        level = jnp.where(row8 == 0, lhi, jnp.where(row8 == 1, lmid, jnp.where(row8 == 2, llo, 0.0)))
        yy[i] = jnp.concatenate([hi, hi, mid, hi, lo, mid, level, zeros], axis=0).astype(bf16)
        tgt_w[i] = sum_weights(v, row8)
        return carry

    lax.fori_loop(0, slots, prepare_tgt, 0, unroll=2)

    top = rows_of((8, LANES)) < 4

    def fold(s):
        s = s[:8] + s[8:]
        return jnp.where(top, s[:, :LANES], pltpu.roll(s[:, LANES:], 4, 0))

    def exponent(k):
        return lax.dot_general(
            yy[pair_slot[k]],
            xx[pair_src[k]],
            (((0,), (0,)), ((), ())),
            preferred_element_type=f32,
        )

    def pair(k, expo):
        later = exponent(jnp.minimum(k + 1, pairs - 1))
        kern = jnp.exp2(expo)
        hi = kern.astype(bf16)
        lo = (kern - hi.astype(f32)).astype(bf16)
        w, a = tgt_w[pair_slot[k]], src_w[pair_src[k]]
        s = jnp.dot(w, hi, preferred_element_type=f32) + jnp.dot(w, lo, preferred_element_type=f32)
        nt = (((1,), (1,)), ((), ()))
        t = lax.dot_general(a, hi, nt, preferred_element_type=f32) + lax.dot_general(
            a, lo, nt, preferred_element_type=f32
        )
        src_parts[pl.ds(pl.multiple_of(k * 8, 8), 8), :] = fold(s)
        tgt_parts[pl.ds(pl.multiple_of(k * 8, 8), 8), :] = fold(t)
        return later

    lax.fori_loop(0, pairs, pair, exponent(0), unroll=4)

    def combine(names, count, parts, put):
        at = lax.broadcasted_iota(jnp.int32, (count, pairs), 1)
        pick = (jnp.broadcast_to(names[...], (count, pairs)) == rows_of((count, pairs))) & (
            at < pair_count[0]
        )
        pick = jnp.where(pick, 1.0, 0.0).astype(bf16)
        for r in range(8):
            parts_r = jnp.concatenate(split3(parts[pl.ds(r, pairs, stride=8), :]), axis=1)
            s = jnp.dot(pick, parts_r.astype(bf16), preferred_element_type=f32)
            put[pl.ds(r, count, stride=8), :] = (
                s[:, :LANES] + s[:, LANES : 2 * LANES] + s[:, 2 * LANES :]
            )

    combine(slot_row, slots, tgt_parts, tgt_send)

    def of_owner(ref, r):
        return ref.at[pl.ds(pl.multiple_of(r * (8 * REQ), 8 * REQ), 8 * REQ), :]

    t_copies = [
        send(
            of_owner(tgt_send, at_r(d)),
            tgt_back.at[mr],
            t_send.at[d],
            t_recv.at[d],
            in_clus(at_r(d)),
        )
        for d in range(1, n_clus)
    ]
    for copy in t_copies:
        copy.start()

    combine(src_row, n_tgt * OWN, src_parts, src_send)

    def of_group(ref, t):
        return ref.at[pl.ds(pl.multiple_of(t * (8 * OWN), 8 * OWN), 8 * OWN), :]

    r_copies = [
        send(
            of_group(src_send, at_t(d)),
            src_back.at[mt],
            r_send.at[d],
            r_recv.at[d],
            in_tgt(at_t(d)),
        )
        for d in range(1, n_tgt)
    ]
    for copy in r_copies:
        copy.start()
    tgt_back[mr] = of_owner(tgt_send, mr)[...]
    src_back[mt] = of_group(src_send, mt)[...]

    def finish(xs, weight_ref, pot_ref, live, out_pos, out_weight):
        us = get_tiles(total)
        for c in range(3):
            out_pos[c] = jnp.where(live, xs[c] * us[3] - us[c], 0.0)
        out_weight[...] = jnp.where(
            live, pot_ref[...] - ENTROPIC * us[3] / weight_ref[...], 0.0
        )

    for copy in b_copies + t_copies:
        copy.wait_recv()

    def add_tgt(r, sums):
        sums = list(sums)
        for m in range(REQ):
            which = jnp.broadcast_to(back_req[r, m : m + 1, :], (8, LANES))
            tile = tgt_back[r, m * 8 : m * 8 + 8, :]
            for b in range(OWN):
                sums[b] = sums[b] + jnp.where(which == b, tile, 0.0)
        return tuple(sums)

    sums = lax.fori_loop(0, n_clus, add_tgt, tuple(jnp.zeros((8, LANES), f32) for _ in range(OWN)))
    for b in range(OWN):
        total[b * 8 : b * 8 + 8, :] = sums[b]
    finish(txs, tgt_weight, tgt_pot, tlive, out_tgt_pos, out_tgt_weight)

    for copy in r_copies:
        copy.wait_recv()
    whole = src_back[0]
    for t in range(1, n_tgt):
        whole = whole + src_back[t]
    total[...] = whole
    finish(sxs, src_weight, src_pot, slive, out_src_pos, out_src_weight)

    for copy in x_copies + q_copies + s_copies + z_copies + b_copies + t_copies + r_copies:
        copy.wait_send()


def shards(
    dims,
    src_pos,
    src_weight,
    src_pot,
    src_count,
    tgt_pos,
    tgt_weight,
    tgt_pot,
    tgt_count,
    requests,
    pair_src,
    pair_slot,
    pair_count,
):
    nx, nz, ny, nc = dims
    n_tgt, n_clus = ny * nc, nx * nz
    slots = n_clus * REQ
    pairs = pair_src.shape[0]
    quarters = 2 * OWN

    def tall(v):
        return v.reshape(*v.shape[:-1], quarters, LANES)

    smem = pl.BlockSpec(memory_space=pltpu.SMEM)
    vmem = pl.BlockSpec(memory_space=pltpu.VMEM)
    dma = pltpu.SemaphoreType.DMA
    outs = pl.pallas_call(
        functools.partial(kernel, dims),
        out_shape=[
            jax.ShapeDtypeStruct((3, quarters, LANES), f32),
            jax.ShapeDtypeStruct((quarters, LANES), f32),
        ]
        * 2,
        in_specs=[smem] * 6 + [vmem] * 8,
        out_specs=[vmem] * 4,
        scratch_shapes=[
            pltpu.VMEM((n_tgt, 8 * OWN, LANES), f32),
            pltpu.VMEM((nx, 8 * OWN, LANES), f32),
            pltpu.VMEM((nz, nx, REQ, 8, LANES), f32),
            pltpu.VMEM((nz, nx, REQ, 8, LANES), f32),
            pltpu.VMEM((nz, nx, REQ, LANES), jnp.int32),
            pltpu.VMEM((nz, nx, REQ, LANES), jnp.int32),
            pltpu.VMEM((n_clus, REQ, LANES), jnp.int32),
            pltpu.VMEM((n_tgt * OWN, 64, BLK), bf16),
            pltpu.VMEM((slots, 64, BLK), bf16),
            pltpu.VMEM((n_tgt * OWN, 16, BLK), bf16),
            pltpu.VMEM((slots, 16, BLK), bf16),
            pltpu.VMEM((pairs * 8, LANES), f32),
            pltpu.VMEM((pairs * 8, LANES), f32),
            pltpu.VMEM((n_tgt * OWN * 8, LANES), f32),
            pltpu.VMEM((slots * 8, LANES), f32),
            pltpu.VMEM((n_tgt, 8 * OWN, LANES), f32),
            pltpu.VMEM((n_clus, 8 * REQ, LANES), f32),
            pltpu.VMEM((8 * OWN, LANES), f32),
            dma((nx,)),
            dma((nx,)),
            dma((nz,)),
            dma((nz,)),
            dma((n_tgt,)),
            dma((n_tgt,)),
            dma((nz,)),
            dma((nz,)),
            dma((n_clus,)),
            dma((n_clus,)),
            dma((n_clus,)),
            dma((n_clus,)),
            dma((n_tgt,)),
            dma((n_tgt,)),
        ],
        compiler_params=pltpu.CompilerParams(
            collective_id=0, has_side_effects=True, vmem_limit_bytes=32 << 20
        ),
    )(
        pair_src,
        pair_slot,
        pair_count,
        requests,
        src_count,
        tgt_count,
        pair_src[None, :],
        pair_slot[None, :],
        tall(src_pos),
        tall(src_weight),
        tall(src_pot),
        tall(tgt_pos),
        tall(tgt_weight),
        tall(tgt_pot),
    )
    return tuple(v.reshape(*v.shape[:-2], quarters * LANES) for v in outs)


def solution(mesh):
    n_clus, n_tgt = mesh.shape["clus"], mesh.shape["tgt"]
    nx = math.isqrt(n_clus)
    dims = (nx, n_clus // nx, n_tgt // 2, 2)
    torus = Mesh(mesh.devices.reshape(dims), AXES)
    wide, flat = P(None, AXES), P(AXES)
    return jax.shard_map(
        functools.partial(shards, dims),
        mesh=torus,
        in_specs=(
            wide,
            flat,
            flat,
            flat,
            wide,
            flat,
            flat,
            flat,
            P(AXES, None),
            flat,
            flat,
            flat,
        ),
        out_specs=(wide, flat, wide, flat),
        check_vma=False,
    )
```

```python
import functools
import math

import jax
import jax.numpy as jnp
from jax import lax
from jax.experimental import pallas as pl
from jax.experimental.pallas import tpu as pltpu
from jax.sharding import Mesh
from jax.sharding import PartitionSpec as P

AXES = ("x", "z", "y", "core")
MESH = pl.DeviceIdType.MESH
BLK = 256
LANES = 128
OWN = 8
REQ = 2
ENTROPIC = 0.05
SCALE = 1.0 / (ENTROPIC * math.log(2.0))
DEAD = -1.0e4
VMEM = 67043328
f32 = jnp.float32
bf16 = jnp.bfloat16


def split3(v):
    hi = v.astype(bf16).astype(f32)
    rest = v - hi
    mid = rest.astype(bf16).astype(f32)
    return hi, mid, rest - mid


def rows_of(shape):
    return lax.broadcasted_iota(jnp.int32, shape, 0)


def pack(pos_ref, weight_ref, pot_ref, count_ref):
    quarters = weight_ref.shape[0]
    row = rows_of((quarters, LANES))
    lane = lax.broadcasted_iota(jnp.int32, (quarters, LANES), 1)
    counts = jnp.zeros((quarters, LANES), jnp.int32)
    for b in range(OWN):
        counts = jnp.where((row >> 1) == b, count_ref[b], counts)
    live = ((row & 1) * LANES + lane) < counts
    xs = [
        jnp.concatenate(
            [pos_ref[c : c + 1, q * LANES : q * LANES + LANES] for q in range(quarters)], axis=0
        )
        - 0.5
        for c in range(3)
    ]
    square = xs[0] * xs[0] + xs[1] * xs[1] + xs[2] * xs[2]
    level = SCALE * (pot_ref[...] - 0.5 * square) + jnp.log(weight_ref[...]) * (1.0 / math.log(2.0))
    return xs, jnp.where(live, level, DEAD), live


def put_tiles(tiles, comps):
    for c, comp in enumerate(comps):
        tiles[pl.ds(c, 2 * OWN, stride=4), :] = comp


def get_tiles(tiles):
    return [tiles[pl.ds(c, 2 * OWN, stride=4), :] for c in range(4)]


def unfold(tile):
    return jnp.concatenate([tile, pltpu.roll(tile, 4, 0)], axis=1)


def sum_weights(v, row):
    w = jnp.where((row & 3) == 3, 1.0, v)
    hi = w.astype(bf16).astype(f32)
    return jnp.concatenate([hi, w - hi], axis=0).astype(bf16)


def kernel(
    dims,
    inputs,
    out_src,
    out_tgt,
    held,
    in_sem,
    src_all,
    row_all,
    tgt_all,
    chosen,
    own_req,
    z_req,
    back_req,
    xx,
    yy,
    src_w,
    tgt_w,
    src_parts,
    tgt_parts,
    src_send,
    tgt_send,
    src_back,
    tgt_back,
    total,
    x_send,
    x_recv,
    q_send,
    q_recv,
    s_send,
    s_recv,
    z_send,
    z_recv,
    b_send,
    b_recv,
    t_send,
    t_recv,
    r_send,
    r_recv,
):
    nx, nz, ny, nc = dims
    n_tgt, n_clus = ny * nc, nx * nz
    slots = n_clus * REQ
    mx, mz, my, mc = (lax.axis_index(a) for a in AXES)
    mt, mr = my * nc + mc, mx * nz + mz

    def at_x(d):
        return lax.rem(mx + d, nx)

    def at_z(d):
        return lax.rem(mz + d, nz)

    def at_t(d):
        return lax.rem(mt + d, n_tgt)

    def at_r(d):
        return lax.rem(mr + d, n_clus)

    def in_tgt(t):
        return (mx, mz, t // nc, lax.rem(t, nc))

    def in_clus(r):
        return (r // nz, lax.rem(r, nz), my, mc)

    def send(src, dst, send_sem, recv_sem, device):
        return pltpu.make_async_remote_copy(
            src_ref=src,
            dst_ref=dst,
            send_sem=send_sem,
            recv_sem=recv_sem,
            device_id=device,
            device_id_type=MESH,
        )

    barrier = pltpu.get_barrier_semaphore()
    for d in range(1, nx):
        pl.semaphore_signal(barrier, inc=1, device_id=(at_x(d), mz, my, mc), device_id_type=MESH)
    for d in range(1, nz):
        pl.semaphore_signal(barrier, inc=1, device_id=(mx, at_z(d), my, mc), device_id_type=MESH)
    for d in range(1, n_tgt):
        pl.semaphore_signal(barrier, inc=1, device_id=in_tgt(at_t(d)), device_id_type=MESH)

    loads = [
        pltpu.make_async_copy(src, dst, in_sem.at[i])
        for i, (src, dst) in enumerate(zip(inputs, held))
    ]
    for load in loads:
        load.start()
    for load in loads:
        load.wait()
    (
        tgt_pos,
        tgt_weight,
        tgt_pot,
        tgt_count,
        requests,
        src_pos,
        src_weight,
        src_pot,
        src_count,
        pair_src,
        pair_slot,
        pair_count,
        src_row,
        slot_row,
    ) = held
    pairs = pair_src.shape[0]
    txs, tlevel, tlive = pack(tgt_pos, tgt_weight, tgt_pot, tgt_count)
    put_tiles(row_all.at[mx], txs + [tlevel])
    sxs, slevel, slive = pack(src_pos, src_weight, src_pot, src_count)
    put_tiles(src_all.at[mt], sxs + [slevel])
    for r in range(n_clus):
        for m in range(REQ):
            own_req[r % nz, r // nz, m] = jnp.full((LANES,), requests[m, r], jnp.int32)

    pl.semaphore_wait(barrier, nx - 1 + nz - 1 + n_tgt - 1)

    x_copies = [
        send(row_all.at[mx], row_all.at[mx], x_send.at[d], x_recv.at[d], (at_x(d), mz, my, mc))
        for d in range(1, nx)
    ]
    q_copies = [
        send(own_req.at[at_z(d)], z_req.at[mz], q_send.at[d], q_recv.at[d], (mx, at_z(d), my, mc))
        for d in range(1, nz)
    ]
    s_copies = [
        send(src_all.at[mt], src_all.at[mt], s_send.at[d], s_recv.at[d], in_tgt(at_t(d)))
        for d in range(1, n_tgt)
    ]
    for copy in x_copies + q_copies + s_copies:
        copy.start()
    z_req[mz] = own_req[mz]

    for copy in q_copies + x_copies:
        copy.wait_recv()

    def choose(asked, put):
        for x in range(nx):
            blocks = [row_all[x, b * 8 : b * 8 + 8, :] for b in range(OWN)]
            for m in range(REQ):
                which = jnp.broadcast_to(z_req[asked, x, m : m + 1, :], (8, LANES))
                tile = blocks[0]
                for b in range(1, OWN):
                    tile = jnp.where(which == b, blocks[b], tile)
                put(x, m, tile)

    z_copies = []
    for d in range(1, nz):

        def put(x, m, tile, d=d):
            chosen[d, x, m] = tile

        choose(at_z(d), put)
        copy = send(
            chosen.at[d], tgt_all.at[mz], z_send.at[d], z_recv.at[d], (mx, at_z(d), my, mc)
        )
        copy.start()
        z_copies.append(copy)

    def put_own(x, m, tile):
        tgt_all[mz, x, m] = tile

    choose(mz, put_own)

    row8 = rows_of((8, BLK))
    ones3 = jnp.where(row8 < 3, 1.0, 0.0)
    zeros = jnp.zeros((8, BLK), f32)

    for copy in s_copies:
        copy.wait_recv()

    def prepare_src(i, carry):
        v = unfold(src_all[i // OWN, pl.ds(pl.multiple_of(lax.rem(i, OWN) * 8, 8), 8), :])
        hi, mid, lo = split3(v)
        xx[i] = jnp.concatenate([hi, mid, hi, lo, hi, mid, ones3, zeros], axis=0).astype(bf16)
        src_w[i] = sum_weights(v, row8)
        return carry

    lax.fori_loop(0, n_tgt * OWN, prepare_src, 0, unroll=2)

    for copy in z_copies:
        copy.wait_recv()

    b_copies = [
        send(
            own_req.at[lax.rem(at_r(d), nz), at_r(d) // nz],
            back_req.at[mr],
            b_send.at[d],
            b_recv.at[d],
            in_clus(at_r(d)),
        )
        for d in range(1, n_clus)
    ]
    for copy in b_copies:
        copy.start()
    back_req[mr] = own_req[mz, mx]

    def prepare_tgt(i, carry):
        r, m = i // REQ, lax.rem(i, REQ)
        v = unfold(tgt_all[lax.rem(r, nz), r // nz, m])
        hi, mid, lo = split3(jnp.where(row8 < 3, SCALE * v, jnp.where(row8 == 3, 1.0, 0.0)))
        lhi, lmid, llo = split3(jnp.broadcast_to(v[3:4, :], (8, BLK)))
        level = jnp.where(row8 == 0, lhi, jnp.where(row8 == 1, lmid, jnp.where(row8 == 2, llo, 0.0)))
        yy[i] = jnp.concatenate([hi, hi, mid, hi, lo, mid, level, zeros], axis=0).astype(bf16)
        tgt_w[i] = sum_weights(v, row8)
        return carry

    lax.fori_loop(0, slots, prepare_tgt, 0, unroll=2)

    top = rows_of((8, LANES)) < 4

    def fold(s):
        s = s[:8] + s[8:]
        return jnp.where(top, s[:, :LANES], pltpu.roll(s[:, LANES:], 4, 0))

    def exponent(k):
        return lax.dot_general(
            yy[pair_slot[k]],
            xx[pair_src[k]],
            (((0,), (0,)), ((), ())),
            preferred_element_type=f32,
        )

    def pair(k, expo):
        later = exponent(jnp.minimum(k + 1, pairs - 1))
        kern = jnp.exp2(expo)
        hi = kern.astype(bf16)
        lo = (kern - hi.astype(f32)).astype(bf16)
        w, a = tgt_w[pair_slot[k]], src_w[pair_src[k]]
        s = jnp.dot(w, hi, preferred_element_type=f32) + jnp.dot(w, lo, preferred_element_type=f32)
        nt = (((1,), (1,)), ((), ()))
        t = lax.dot_general(a, hi, nt, preferred_element_type=f32) + lax.dot_general(
            a, lo, nt, preferred_element_type=f32
        )
        src_parts[pl.ds(pl.multiple_of(k * 8, 8), 8), :] = fold(s)
        tgt_parts[pl.ds(pl.multiple_of(k * 8, 8), 8), :] = fold(t)
        return later

    lax.fori_loop(0, pairs, pair, exponent(0), unroll=4)

    def combine(names, count, parts, put):
        at = lax.broadcasted_iota(jnp.int32, (count, pairs), 1)
        pick = (jnp.broadcast_to(names[...], (count, pairs)) == rows_of((count, pairs))) & (
            at < jnp.broadcast_to(pair_count[...], (count, pairs))
        )
        pick = jnp.where(pick, 1.0, 0.0).astype(bf16)
        for r in range(8):
            parts_r = jnp.concatenate(split3(parts[pl.ds(r, pairs, stride=8), :]), axis=1)
            s = jnp.dot(pick, parts_r.astype(bf16), preferred_element_type=f32)
            put[pl.ds(r, count, stride=8), :] = (
                s[:, :LANES] + s[:, LANES : 2 * LANES] + s[:, 2 * LANES :]
            )

    combine(slot_row, slots, tgt_parts, tgt_send)

    def of_owner(ref, r):
        return ref.at[pl.ds(pl.multiple_of(r * (8 * REQ), 8 * REQ), 8 * REQ), :]

    t_copies = [
        send(
            of_owner(tgt_send, at_r(d)),
            tgt_back.at[mr],
            t_send.at[d],
            t_recv.at[d],
            in_clus(at_r(d)),
        )
        for d in range(1, n_clus)
    ]
    for copy in t_copies:
        copy.start()

    combine(src_row, n_tgt * OWN, src_parts, src_send)

    def of_group(ref, t):
        return ref.at[pl.ds(pl.multiple_of(t * (8 * OWN), 8 * OWN), 8 * OWN), :]

    r_copies = [
        send(
            of_group(src_send, at_t(d)),
            src_back.at[mt],
            r_send.at[d],
            r_recv.at[d],
            in_tgt(at_t(d)),
        )
        for d in range(1, n_tgt)
    ]
    for copy in r_copies:
        copy.start()
    tgt_back[mr] = of_owner(tgt_send, mr)[...]
    src_back[mt] = of_group(src_send, mt)[...]

    def finish(xs, weight_ref, pot_ref, live, out):
        us = get_tiles(total)
        comps = [xs[c] * us[3] - us[c] for c in range(3)]
        comps.append(pot_ref[...] - ENTROPIC * us[3] / weight_ref[...])
        put_tiles(out, [jnp.where(live, comp, 0.0) for comp in comps])

    for copy in b_copies + t_copies:
        copy.wait_recv()

    def add_tgt(r, sums):
        sums = list(sums)
        for m in range(REQ):
            which = jnp.broadcast_to(back_req[r, m : m + 1, :], (8, LANES))
            tile = tgt_back[r, m * 8 : m * 8 + 8, :]
            for b in range(OWN):
                sums[b] = sums[b] + jnp.where(which == b, tile, 0.0)
        return tuple(sums)

    sums = lax.fori_loop(0, n_clus, add_tgt, tuple(jnp.zeros((8, LANES), f32) for _ in range(OWN)))
    for b in range(OWN):
        total[b * 8 : b * 8 + 8, :] = sums[b]
    finish(txs, tgt_weight, tgt_pot, tlive, out_tgt)

    for copy in r_copies:
        copy.wait_recv()
    whole = src_back[0]
    for t in range(1, n_tgt):
        whole = whole + src_back[t]
    total[...] = whole
    finish(sxs, src_weight, src_pot, slive, out_src)

    for copy in x_copies + q_copies + s_copies + z_copies + b_copies + t_copies + r_copies:
        copy.wait_send()


def write_out(sums, src_pos, src_weight, tgt_pos, tgt_weight, held, sem):
    loads = [pltpu.make_async_copy(sums[i], held.at[i], sem.at[i]) for i in range(2)]
    for load in loads:
        load.start()
    for i, (pos, weight) in enumerate(((src_pos, src_weight), (tgt_pos, tgt_weight))):
        loads[i].wait()
        tiles = held.at[i]
        for q in range(2 * OWN):
            pos[:, q * LANES : q * LANES + LANES] = tiles[q * 4 : q * 4 + 3, :]
        weight[...] = tiles[pl.ds(3, 2 * OWN, stride=4), :]


def shards(
    dims,
    src_pos,
    src_weight,
    src_pot,
    src_count,
    tgt_pos,
    tgt_weight,
    tgt_pot,
    tgt_count,
    requests,
    pair_src,
    pair_slot,
    pair_count,
):
    nx, nz, ny, nc = dims
    n_tgt, n_clus = ny * nc, nx * nz
    slots = n_clus * REQ
    pairs = pair_src.shape[0]
    quarters = 2 * OWN

    def tall(v):
        return v.reshape(*v.shape[:-1], quarters, LANES)

    vmem = pl.BlockSpec(memory_space=pltpu.VMEM)
    dma = pltpu.SemaphoreType.DMA
    inputs = [
        tgt_pos,
        tall(tgt_weight),
        tall(tgt_pot),
        tgt_count,
        requests.T,
        src_pos,
        tall(src_weight),
        tall(src_pot),
        src_count,
        pair_src,
        pair_slot,
        pair_count[None, :],
        pair_src[None, :],
        pair_slot[None, :],
    ]
    spaces = [pltpu.SMEM if i in (3, 4, 8, 9, 10) else pltpu.VMEM for i in range(14)]
    tiles = jax.ShapeDtypeStruct((8 * OWN, LANES), f32)
    sums = pl.pallas_call(
        functools.partial(kernel, dims),
        out_shape=[tiles, tiles],
        in_specs=[[pl.BlockSpec(memory_space=pltpu.HBM)] * len(inputs)],
        out_specs=[vmem] * 2,
        scratch_shapes=[
            [space(v.shape, v.dtype) for space, v in zip(spaces, inputs)],
            dma((len(inputs),)),
            pltpu.VMEM((n_tgt, 8 * OWN, LANES), f32),
            pltpu.VMEM((nx, 8 * OWN, LANES), f32),
            pltpu.VMEM((nz, nx, REQ, 8, LANES), f32),
            pltpu.VMEM((nz, nx, REQ, 8, LANES), f32),
            pltpu.VMEM((nz, nx, REQ, LANES), jnp.int32),
            pltpu.VMEM((nz, nx, REQ, LANES), jnp.int32),
            pltpu.VMEM((n_clus, REQ, LANES), jnp.int32),
            pltpu.VMEM((n_tgt * OWN, 64, BLK), bf16),
            pltpu.VMEM((slots, 64, BLK), bf16),
            pltpu.VMEM((n_tgt * OWN, 16, BLK), bf16),
            pltpu.VMEM((slots, 16, BLK), bf16),
            pltpu.VMEM((pairs * 8, LANES), f32),
            pltpu.VMEM((pairs * 8, LANES), f32),
            pltpu.VMEM((n_tgt * OWN * 8, LANES), f32),
            pltpu.VMEM((slots * 8, LANES), f32),
            pltpu.VMEM((n_tgt, 8 * OWN, LANES), f32),
            pltpu.VMEM((n_clus, 8 * REQ, LANES), f32),
            pltpu.VMEM((8 * OWN, LANES), f32),
            dma((nx,)),
            dma((nx,)),
            dma((nz,)),
            dma((nz,)),
            dma((n_tgt,)),
            dma((n_tgt,)),
            dma((nz,)),
            dma((nz,)),
            dma((n_clus,)),
            dma((n_clus,)),
            dma((n_clus,)),
            dma((n_clus,)),
            dma((n_tgt,)),
            dma((n_tgt,)),
        ],
        compiler_params=pltpu.CompilerParams(
            collective_id=0, has_side_effects=True, vmem_limit_bytes=VMEM
        ),
    )(inputs)
    pos = jax.ShapeDtypeStruct((3, quarters * LANES), f32)
    weight = jax.ShapeDtypeStruct((quarters, LANES), f32)
    outs = pl.pallas_call(
        write_out,
        out_shape=[pos, weight, pos, weight],
        in_specs=[[pl.BlockSpec(memory_space=pltpu.HBM)] * 2],
        scratch_shapes=[pltpu.VMEM((2, 8 * OWN, LANES), f32), dma((2,))],
        compiler_params=pltpu.CompilerParams(vmem_limit_bytes=VMEM),
    )(list(sums))
    return outs[0], outs[1].reshape(-1), outs[2], outs[3].reshape(-1)


def solution(mesh):
    n_clus, n_tgt = mesh.shape["clus"], mesh.shape["tgt"]
    nx = math.isqrt(n_clus)
    dims = (nx, n_clus // nx, n_tgt // 2, 2)
    torus = Mesh(mesh.devices.reshape(dims), AXES)
    wide, flat = P(None, AXES), P(AXES)
    return jax.shard_map(
        functools.partial(shards, dims),
        mesh=torus,
        in_specs=(
            wide,
            flat,
            flat,
            flat,
            wide,
            flat,
            flat,
            flat,
            P(AXES, None),
            flat,
            flat,
            flat,
        ),
        out_specs=(wide, flat, wide, flat),
        check_vma=False,
    )
```

```python
import functools
import math

import jax
import jax.numpy as jnp
from jax import lax
from jax.experimental import pallas as pl
from jax.experimental.pallas import tpu as pltpu
from jax.sharding import Mesh
from jax.sharding import PartitionSpec as P

AXES = ("x", "z", "y", "core")
MESH = pl.DeviceIdType.MESH
BLK = 256
LANES = 128
OWN = 8
REQ = 2
ENTROPIC = 0.05
SCALE = 1.0 / (ENTROPIC * math.log(2.0))
DEAD = -1.0e4
VMEM = 67043328
f32 = jnp.float32
bf16 = jnp.bfloat16


def far_first(n):
    return sorted(range(1, n), key=lambda d: (-min(d, n - d), d))


def split3(v):
    hi = v.astype(bf16).astype(f32)
    rest = v - hi
    mid = rest.astype(bf16).astype(f32)
    return hi, mid, rest - mid


def rows_of(shape):
    return lax.broadcasted_iota(jnp.int32, shape, 0)


def pack(pos_ref, weight_ref, pot_ref, count_ref):
    quarters = weight_ref.shape[0]
    row = rows_of((quarters, LANES))
    lane = lax.broadcasted_iota(jnp.int32, (quarters, LANES), 1)
    counts = jnp.zeros((quarters, LANES), jnp.int32)
    for b in range(OWN):
        counts = jnp.where((row >> 1) == b, count_ref[b], counts)
    live = ((row & 1) * LANES + lane) < counts
    xs = [
        jnp.concatenate(
            [pos_ref[c : c + 1, q * LANES : q * LANES + LANES] for q in range(quarters)], axis=0
        )
        - 0.5
        for c in range(3)
    ]
    square = xs[0] * xs[0] + xs[1] * xs[1] + xs[2] * xs[2]
    level = SCALE * (pot_ref[...] - 0.5 * square) + jnp.log(weight_ref[...]) * (1.0 / math.log(2.0))
    return xs, jnp.where(live, level, DEAD), live


def put_tiles(tiles, comps):
    for c, comp in enumerate(comps):
        tiles[pl.ds(c, 2 * OWN, stride=4), :] = comp


def get_tiles(tiles):
    return [tiles[pl.ds(c, 2 * OWN, stride=4), :] for c in range(4)]


def unfold(tile):
    return jnp.concatenate([tile, pltpu.roll(tile, 4, 0)], axis=1)


def sum_weights(v, row):
    w = jnp.where((row & 3) == 3, 1.0, v)
    hi = w.astype(bf16).astype(f32)
    return jnp.concatenate([hi, w - hi], axis=0).astype(bf16)


def kernel(
    dims,
    inputs,
    out_src,
    out_tgt,
    held,
    in_sem,
    src_all,
    row_all,
    tgt_all,
    chosen,
    own_req,
    z_req,
    back_req,
    xx,
    yy,
    src_w,
    tgt_w,
    src_parts,
    tgt_parts,
    src_send,
    tgt_send,
    src_back,
    tgt_back,
    total,
    x_send,
    x_recv,
    q_send,
    q_recv,
    s_send,
    s_recv,
    z_send,
    z_recv,
    b_send,
    b_recv,
    t_send,
    t_recv,
    r_send,
    r_recv,
):
    nx, nz, ny, nc = dims
    n_tgt, n_clus = ny * nc, nx * nz
    slots = n_clus * REQ
    mx, mz, my, mc = (lax.axis_index(a) for a in AXES)
    mt, mr = my * nc + mc, mx * nz + mz

    def at_x(d):
        return lax.rem(mx + d, nx)

    def at_z(d):
        return lax.rem(mz + d, nz)

    def at_t(d):
        return lax.rem(mt + d, n_tgt)

    def at_r(d):
        return lax.rem(mr + d, n_clus)

    def in_tgt(t):
        return (mx, mz, t // nc, lax.rem(t, nc))

    def in_clus(r):
        return (r // nz, lax.rem(r, nz), my, mc)

    def send(src, dst, send_sem, recv_sem, device):
        return pltpu.make_async_remote_copy(
            src_ref=src,
            dst_ref=dst,
            send_sem=send_sem,
            recv_sem=recv_sem,
            device_id=device,
            device_id_type=MESH,
        )

    barrier = pltpu.get_barrier_semaphore()
    for d in range(1, nx):
        pl.semaphore_signal(barrier, inc=1, device_id=(at_x(d), mz, my, mc), device_id_type=MESH)
    for d in range(1, nz):
        pl.semaphore_signal(barrier, inc=1, device_id=(mx, at_z(d), my, mc), device_id_type=MESH)
    for d in range(1, n_tgt):
        pl.semaphore_signal(barrier, inc=1, device_id=in_tgt(at_t(d)), device_id_type=MESH)

    loads = [
        pltpu.make_async_copy(src, dst, in_sem.at[i])
        for i, (src, dst) in enumerate(zip(inputs, held))
    ]
    for load in loads:
        load.start()
    (
        tgt_pos,
        tgt_weight,
        tgt_pot,
        tgt_count,
        requests,
        src_pos,
        src_weight,
        src_pot,
        src_count,
        pair_src,
        pair_slot,
        pair_count,
        src_row,
        slot_row,
    ) = held
    pairs = pair_src.shape[0]

    for load in loads[:5]:
        load.wait()
    txs, tlevel, tlive = pack(tgt_pos, tgt_weight, tgt_pot, tgt_count)
    put_tiles(row_all.at[mx], txs + [tlevel])
    for r in range(n_clus):
        for m in range(REQ):
            own_req[r % nz, r // nz, m] = jnp.full((LANES,), requests[m, r], jnp.int32)

    pl.semaphore_wait(barrier, nx - 1 + nz - 1 + n_tgt - 1)

    q_copies = [
        send(own_req.at[at_z(d)], z_req.at[mz], q_send.at[d], q_recv.at[d], (mx, at_z(d), my, mc))
        for d in far_first(nz)
    ]
    x_copies = [
        send(row_all.at[mx], row_all.at[mx], x_send.at[d], x_recv.at[d], (at_x(d), mz, my, mc))
        for d in far_first(nx)
    ]
    for copy in q_copies + x_copies:
        copy.start()
    z_req[mz] = own_req[mz]
    for load in loads[5:]:
        load.wait()
    sxs, slevel, slive = pack(src_pos, src_weight, src_pot, src_count)
    put_tiles(src_all.at[mt], sxs + [slevel])
    s_copies = [
        send(src_all.at[mt], src_all.at[mt], s_send.at[d], s_recv.at[d], in_tgt(at_t(d)))
        for d in range(1, n_tgt)
    ]
    for copy in s_copies:
        copy.start()

    def choose(x, asked, put):
        blocks = [row_all[x, b * 8 : b * 8 + 8, :] for b in range(OWN)]
        for m in range(REQ):
            which = jnp.broadcast_to(z_req[asked, x, m : m + 1, :], (8, LANES))
            tile = blocks[0]
            for b in range(1, OWN):
                tile = jnp.where(which == b, blocks[b], tile)
            put[m] = tile

    for copy in q_copies:
        copy.wait_recv()
    z_copies = {}
    for dx in [0] + far_first(nx)[::-1]:
        x = lax.rem(mx + nx - dx, nx)
        if dx:
            x_copies[far_first(nx).index(dx)].wait_recv()
        for dz in far_first(nz):
            choose(x, at_z(dz), chosen.at[dz, dx])
            copy = send(
                chosen.at[dz, dx],
                tgt_all.at[mz, x],
                z_send.at[dz, dx],
                z_recv.at[dz, dx],
                (mx, at_z(dz), my, mc),
            )
            copy.start()
            z_copies[dz, dx] = copy
        choose(x, mz, tgt_all.at[mz, x])

    row8 = rows_of((8, BLK))
    ones3 = jnp.where(row8 < 3, 1.0, 0.0)
    zeros = jnp.zeros((8, BLK), f32)

    for copy in s_copies:
        copy.wait_recv()

    def prepare_src(i, carry):
        v = unfold(src_all[i // OWN, pl.ds(pl.multiple_of(lax.rem(i, OWN) * 8, 8), 8), :])
        hi, mid, lo = split3(v)
        xx[i] = jnp.concatenate([hi, mid, hi, lo, hi, mid, ones3, zeros], axis=0).astype(bf16)
        src_w[i] = sum_weights(v, row8)
        return carry

    lax.fori_loop(0, n_tgt * OWN, prepare_src, 0, unroll=2)

    def prepare_tgt(z, dx):
        x = lax.rem(mx + nx - dx, nx)
        for m in range(REQ):
            v = unfold(tgt_all[z, x, m])
            hi, mid, lo = split3(jnp.where(row8 < 3, SCALE * v, jnp.where(row8 == 3, 1.0, 0.0)))
            lhi, lmid, llo = split3(jnp.broadcast_to(v[3:4, :], (8, BLK)))
            level = jnp.where(
                row8 == 0, lhi, jnp.where(row8 == 1, lmid, jnp.where(row8 == 2, llo, 0.0))
            )
            i = (x * nz + z) * REQ + m
            yy[i] = jnp.concatenate([hi, hi, mid, hi, lo, mid, level, zeros], axis=0).astype(bf16)
            tgt_w[i] = sum_weights(v, row8)

    for dz in [0] + far_first(nz)[::-1]:
        for dx in [0] + far_first(nx)[::-1]:
            if dz:
                z_copies[dz, dx].wait_recv()
            prepare_tgt(lax.rem(mz + nz - dz, nz), dx)

    b_copies = [
        send(
            own_req.at[lax.rem(at_r(d), nz), at_r(d) // nz],
            back_req.at[mr],
            b_send.at[d],
            b_recv.at[d],
            in_clus(at_r(d)),
        )
        for d in range(1, n_clus)
    ]
    for copy in b_copies:
        copy.start()
    back_req[mr] = own_req[mz, mx]

    top = rows_of((8, LANES)) < 4

    def fold(s):
        s = s[:8] + s[8:]
        return jnp.where(top, s[:, :LANES], pltpu.roll(s[:, LANES:], 4, 0))

    def exponent(k):
        return lax.dot_general(
            yy[pair_slot[k]],
            xx[pair_src[k]],
            (((0,), (0,)), ((), ())),
            preferred_element_type=f32,
        )

    def pair(k, expo):
        later = exponent(jnp.minimum(k + 1, pairs - 1))
        kern = jnp.exp2(expo)
        hi = kern.astype(bf16)
        lo = (kern - hi.astype(f32)).astype(bf16)
        w, a = tgt_w[pair_slot[k]], src_w[pair_src[k]]
        s = jnp.dot(w, hi, preferred_element_type=f32) + jnp.dot(w, lo, preferred_element_type=f32)
        nt = (((1,), (1,)), ((), ()))
        t = lax.dot_general(a, hi, nt, preferred_element_type=f32) + lax.dot_general(
            a, lo, nt, preferred_element_type=f32
        )
        src_parts[pl.ds(pl.multiple_of(k * 8, 8), 8), :] = fold(s)
        tgt_parts[pl.ds(pl.multiple_of(k * 8, 8), 8), :] = fold(t)
        return later

    lax.fori_loop(0, pairs, pair, exponent(0), unroll=4)

    def combine(names, count, parts, put):
        at = lax.broadcasted_iota(jnp.int32, (count, pairs), 1)
        pick = (jnp.broadcast_to(names[...], (count, pairs)) == rows_of((count, pairs))) & (
            at < jnp.broadcast_to(pair_count[...], (count, pairs))
        )
        pick = jnp.where(pick, 1.0, 0.0).astype(bf16)
        for r in range(8):
            parts_r = jnp.concatenate(split3(parts[pl.ds(r, pairs, stride=8), :]), axis=1)
            s = jnp.dot(pick, parts_r.astype(bf16), preferred_element_type=f32)
            put[pl.ds(r, count, stride=8), :] = (
                s[:, :LANES] + s[:, LANES : 2 * LANES] + s[:, 2 * LANES :]
            )

    combine(slot_row, slots, tgt_parts, tgt_send)

    def of_owner(ref, r):
        return ref.at[pl.ds(pl.multiple_of(r * (8 * REQ), 8 * REQ), 8 * REQ), :]

    t_copies = [
        send(
            of_owner(tgt_send, at_r(d)),
            tgt_back.at[mr],
            t_send.at[d],
            t_recv.at[d],
            in_clus(at_r(d)),
        )
        for d in range(1, n_clus)
    ]
    for copy in t_copies:
        copy.start()

    combine(src_row, n_tgt * OWN, src_parts, src_send)

    def of_group(ref, t):
        return ref.at[pl.ds(pl.multiple_of(t * (8 * OWN), 8 * OWN), 8 * OWN), :]

    r_copies = [
        send(
            of_group(src_send, at_t(d)),
            src_back.at[mt],
            r_send.at[d],
            r_recv.at[d],
            in_tgt(at_t(d)),
        )
        for d in range(1, n_tgt)
    ]
    for copy in r_copies:
        copy.start()
    tgt_back[mr] = of_owner(tgt_send, mr)[...]
    src_back[mt] = of_group(src_send, mt)[...]

    def finish(xs, weight_ref, pot_ref, live, out):
        us = get_tiles(total)
        comps = [xs[c] * us[3] - us[c] for c in range(3)]
        comps.append(pot_ref[...] - ENTROPIC * us[3] / weight_ref[...])
        put_tiles(out, [jnp.where(live, comp, 0.0) for comp in comps])

    for copy in b_copies + t_copies:
        copy.wait_recv()

    def add_tgt(r, sums):
        sums = list(sums)
        for m in range(REQ):
            which = jnp.broadcast_to(back_req[r, m : m + 1, :], (8, LANES))
            tile = tgt_back[r, m * 8 : m * 8 + 8, :]
            for b in range(OWN):
                sums[b] = sums[b] + jnp.where(which == b, tile, 0.0)
        return tuple(sums)

    sums = lax.fori_loop(0, n_clus, add_tgt, tuple(jnp.zeros((8, LANES), f32) for _ in range(OWN)))
    for b in range(OWN):
        total[b * 8 : b * 8 + 8, :] = sums[b]
    finish(txs, tgt_weight, tgt_pot, tlive, out_tgt)

    for copy in r_copies:
        copy.wait_recv()
    whole = src_back[0]
    for t in range(1, n_tgt):
        whole = whole + src_back[t]
    total[...] = whole
    finish(sxs, src_weight, src_pot, slive, out_src)

    for copy in (
        x_copies + q_copies + s_copies + list(z_copies.values()) + b_copies + t_copies + r_copies
    ):
        copy.wait_send()


def write_out(src, tgt, src_pos, src_weight, tgt_pos, tgt_weight):
    for tiles, pos, weight in ((src, src_pos, src_weight), (tgt, tgt_pos, tgt_weight)):
        for q in range(2 * OWN):
            pos[:, q * LANES : q * LANES + LANES] = tiles[q * 4 : q * 4 + 3, :]
        weight[...] = tiles[pl.ds(3, 2 * OWN, stride=4), :]


def shards(
    dims,
    src_pos,
    src_weight,
    src_pot,
    src_count,
    tgt_pos,
    tgt_weight,
    tgt_pot,
    tgt_count,
    requests,
    pair_src,
    pair_slot,
    pair_count,
):
    nx, nz, ny, nc = dims
    n_tgt, n_clus = ny * nc, nx * nz
    slots = n_clus * REQ
    pairs = pair_src.shape[0]
    quarters = 2 * OWN

    def tall(v):
        return v.reshape(*v.shape[:-1], quarters, LANES)

    vmem = pl.BlockSpec(memory_space=pltpu.VMEM)
    dma = pltpu.SemaphoreType.DMA
    inputs = [
        tgt_pos,
        tall(tgt_weight),
        tall(tgt_pot),
        tgt_count,
        requests.T,
        src_pos,
        tall(src_weight),
        tall(src_pot),
        src_count,
        pair_src,
        pair_slot,
        pair_count[None, :],
        pair_src[None, :],
        pair_slot[None, :],
    ]
    spaces = [pltpu.SMEM if i in (3, 4, 8, 9, 10) else pltpu.VMEM for i in range(14)]
    tiles = jax.ShapeDtypeStruct((8 * OWN, LANES), f32)
    sums = pl.pallas_call(
        functools.partial(kernel, dims),
        out_shape=[tiles, tiles],
        in_specs=[[pl.BlockSpec(memory_space=pltpu.HBM)] * len(inputs)],
        out_specs=[vmem] * 2,
        scratch_shapes=[
            [space(v.shape, v.dtype) for space, v in zip(spaces, inputs)],
            dma((len(inputs),)),
            pltpu.VMEM((n_tgt, 8 * OWN, LANES), f32),
            pltpu.VMEM((nx, 8 * OWN, LANES), f32),
            pltpu.VMEM((nz, nx, REQ, 8, LANES), f32),
            pltpu.VMEM((nz, nx, REQ, 8, LANES), f32),
            pltpu.VMEM((nz, nx, REQ, LANES), jnp.int32),
            pltpu.VMEM((nz, nx, REQ, LANES), jnp.int32),
            pltpu.VMEM((n_clus, REQ, LANES), jnp.int32),
            pltpu.VMEM((n_tgt * OWN, 64, BLK), bf16),
            pltpu.VMEM((slots, 64, BLK), bf16),
            pltpu.VMEM((n_tgt * OWN, 16, BLK), bf16),
            pltpu.VMEM((slots, 16, BLK), bf16),
            pltpu.VMEM((pairs * 8, LANES), f32),
            pltpu.VMEM((pairs * 8, LANES), f32),
            pltpu.VMEM((n_tgt * OWN * 8, LANES), f32),
            pltpu.VMEM((slots * 8, LANES), f32),
            pltpu.VMEM((n_tgt, 8 * OWN, LANES), f32),
            pltpu.VMEM((n_clus, 8 * REQ, LANES), f32),
            pltpu.VMEM((8 * OWN, LANES), f32),
            dma((nx,)),
            dma((nx,)),
            dma((nz,)),
            dma((nz,)),
            dma((n_tgt,)),
            dma((n_tgt,)),
            dma((nz, nx)),
            dma((nz, nx)),
            dma((n_clus,)),
            dma((n_clus,)),
            dma((n_clus,)),
            dma((n_clus,)),
            dma((n_tgt,)),
            dma((n_tgt,)),
        ],
        compiler_params=pltpu.CompilerParams(
            collective_id=0, has_side_effects=True, vmem_limit_bytes=48 << 20
        ),
    )(
        [
            v if v.size == 1 else pltpu.with_memory_space_constraint(v, pltpu.HBM)
            for v in inputs
        ]
    )
    pos = jax.ShapeDtypeStruct((3, quarters * LANES), f32)
    weight = jax.ShapeDtypeStruct((quarters, LANES), f32)
    outs = pl.pallas_call(
        write_out,
        out_shape=[pos, weight, pos, weight],
        in_specs=[vmem] * 2,
        compiler_params=pltpu.CompilerParams(vmem_limit_bytes=4 << 20),
    )(*sums)
    return outs[0], outs[1].reshape(-1), outs[2], outs[3].reshape(-1)


def solution(mesh):
    n_clus, n_tgt = mesh.shape["clus"], mesh.shape["tgt"]
    nx = math.isqrt(n_clus)
    dims = (nx, n_clus // nx, n_tgt // 2, 2)
    torus = Mesh(mesh.devices.reshape(dims), AXES)
    wide, flat = P(None, AXES), P(AXES)
    return jax.shard_map(
        functools.partial(shards, dims),
        mesh=torus,
        in_specs=(
            wide,
            flat,
            flat,
            flat,
            wide,
            flat,
            flat,
            flat,
            P(AXES, None),
            flat,
            flat,
            flat,
        ),
        out_specs=(wide, flat, wide, flat),
        check_vma=False,
    )
```

```python
import functools
import math

import jax
import jax.numpy as jnp
from jax import lax
from jax.experimental import pallas as pl
from jax.experimental.pallas import tpu as pltpu
from jax.sharding import Mesh
from jax.sharding import PartitionSpec as P

AXES = ("x", "z", "y", "core")
MESH = pl.DeviceIdType.MESH
BLK = 256
LANES = 128
OWN = 8
REQ = 2
ENTROPIC = 0.05
SCALE = 1.0 / (ENTROPIC * math.log(2.0))
DEAD = -1.0e4
VMEM = 67043328
f32 = jnp.float32
bf16 = jnp.bfloat16
f8 = jnp.float8_e4m3fn
LO = 2.0**13


def far_first(n):
    return sorted(range(1, n), key=lambda d: (-min(d, n - d), d))


def split3(v):
    hi = v.astype(bf16).astype(f32)
    rest = v - hi
    mid = rest.astype(bf16).astype(f32)
    return hi, mid, rest - mid


def rows_of(shape):
    return lax.broadcasted_iota(jnp.int32, shape, 0)


def pack(pos_ref, weight_ref, pot_ref, count_ref):
    quarters = weight_ref.shape[0]
    row = rows_of((quarters, LANES))
    lane = lax.broadcasted_iota(jnp.int32, (quarters, LANES), 1)
    counts = jnp.zeros((quarters, LANES), jnp.int32)
    for b in range(OWN):
        counts = jnp.where((row >> 1) == b, count_ref[b], counts)
    live = ((row & 1) * LANES + lane) < counts
    xs = [
        jnp.concatenate(
            [pos_ref[c : c + 1, q * LANES : q * LANES + LANES] for q in range(quarters)], axis=0
        )
        - 0.5
        for c in range(3)
    ]
    square = xs[0] * xs[0] + xs[1] * xs[1] + xs[2] * xs[2]
    level = SCALE * (pot_ref[...] - 0.5 * square) + jnp.log(weight_ref[...]) * (1.0 / math.log(2.0))
    return xs, jnp.where(live, level, DEAD), live


def put_tiles(tiles, comps):
    for c, comp in enumerate(comps):
        tiles[pl.ds(c, 2 * OWN, stride=4), :] = comp


def get_tiles(tiles):
    return [tiles[pl.ds(c, 2 * OWN, stride=4), :] for c in range(4)]


def unfold(tile):
    return jnp.concatenate([tile, pltpu.roll(tile, 4, 0)], axis=1)


def sum_weights(v, row):
    w = jnp.where((row & 3) == 3, 1.0, v)
    hi = w.astype(bf16).astype(f32)
    coarse = jnp.concatenate([w, jnp.zeros((24, BLK), f32)], axis=0).astype(f8)
    return jnp.concatenate([hi, w - hi], axis=0).astype(bf16), coarse


def kernel(
    dims,
    inputs,
    out_src,
    out_tgt,
    held,
    in_sem,
    src_all,
    row_all,
    tgt_all,
    chosen,
    own_req,
    z_req,
    back_req,
    xx,
    yy,
    src_w,
    tgt_w,
    src_w8,
    tgt_w8,
    src_parts,
    tgt_parts,
    src_send,
    tgt_send,
    src_back,
    tgt_back,
    total,
    x_send,
    x_recv,
    q_send,
    q_recv,
    s_send,
    s_recv,
    z_send,
    z_recv,
    b_send,
    b_recv,
    t_send,
    t_recv,
    r_send,
    r_recv,
):
    nx, nz, ny, nc = dims
    n_tgt, n_clus = ny * nc, nx * nz
    slots = n_clus * REQ
    mx, mz, my, mc = (lax.axis_index(a) for a in AXES)
    mt, mr = my * nc + mc, mx * nz + mz

    def at_x(d):
        return lax.rem(mx + d, nx)

    def at_z(d):
        return lax.rem(mz + d, nz)

    def at_t(d):
        return lax.rem(mt + d, n_tgt)

    def at_r(d):
        return lax.rem(mr + d, n_clus)

    def in_tgt(t):
        return (mx, mz, t // nc, lax.rem(t, nc))

    def in_clus(r):
        return (r // nz, lax.rem(r, nz), my, mc)

    def send(src, dst, send_sem, recv_sem, device):
        return pltpu.make_async_remote_copy(
            src_ref=src,
            dst_ref=dst,
            send_sem=send_sem,
            recv_sem=recv_sem,
            device_id=device,
            device_id_type=MESH,
        )

    barrier = pltpu.get_barrier_semaphore()
    for d in range(1, nx):
        pl.semaphore_signal(barrier, inc=1, device_id=(at_x(d), mz, my, mc), device_id_type=MESH)
    for d in range(1, nz):
        pl.semaphore_signal(barrier, inc=1, device_id=(mx, at_z(d), my, mc), device_id_type=MESH)
    for d in range(1, n_tgt):
        pl.semaphore_signal(barrier, inc=1, device_id=in_tgt(at_t(d)), device_id_type=MESH)

    loads = [
        pltpu.make_async_copy(src, dst, in_sem.at[i])
        for i, (src, dst) in enumerate(zip(inputs, held))
    ]
    for load in loads:
        load.start()
    (
        tgt_pos,
        tgt_weight,
        tgt_pot,
        tgt_count,
        requests,
        src_pos,
        src_weight,
        src_pot,
        src_count,
        pair_src,
        pair_slot,
        pair_count,
        src_row,
        slot_row,
    ) = held
    pairs = pair_src.shape[0]

    for load in loads[:5]:
        load.wait()
    txs, tlevel, tlive = pack(tgt_pos, tgt_weight, tgt_pot, tgt_count)
    put_tiles(row_all.at[mx], txs + [tlevel])
    for r in range(n_clus):
        for m in range(REQ):
            own_req[r % nz, r // nz, m] = jnp.full((LANES,), requests[m, r], jnp.int32)

    pl.semaphore_wait(barrier, nx - 1 + nz - 1 + n_tgt - 1)

    q_copies = [
        send(own_req.at[at_z(d)], z_req.at[mz], q_send.at[d], q_recv.at[d], (mx, at_z(d), my, mc))
        for d in far_first(nz)
    ]
    x_copies = [
        send(row_all.at[mx], row_all.at[mx], x_send.at[d], x_recv.at[d], (at_x(d), mz, my, mc))
        for d in far_first(nx)
    ]
    for copy in q_copies + x_copies:
        copy.start()
    z_req[mz] = own_req[mz]
    for load in loads[5:]:
        load.wait()
    sxs, slevel, slive = pack(src_pos, src_weight, src_pot, src_count)
    put_tiles(src_all.at[mt], sxs + [slevel])
    s_copies = [
        send(src_all.at[mt], src_all.at[mt], s_send.at[d], s_recv.at[d], in_tgt(at_t(d)))
        for d in range(1, n_tgt)
    ]
    for copy in s_copies:
        copy.start()

    def choose(x, asked, put):
        blocks = [row_all[x, b * 8 : b * 8 + 8, :] for b in range(OWN)]
        for m in range(REQ):
            which = jnp.broadcast_to(z_req[asked, x, m : m + 1, :], (8, LANES))
            tile = blocks[0]
            for b in range(1, OWN):
                tile = jnp.where(which == b, blocks[b], tile)
            put[m] = tile

    for copy in q_copies:
        copy.wait_recv()
    z_copies = {}
    for dx in [0] + far_first(nx)[::-1]:
        x = lax.rem(mx + nx - dx, nx)
        if dx:
            x_copies[far_first(nx).index(dx)].wait_recv()
        for dz in far_first(nz):
            choose(x, at_z(dz), chosen.at[dz, dx])
            copy = send(
                chosen.at[dz, dx],
                tgt_all.at[mz, x],
                z_send.at[dz, dx],
                z_recv.at[dz, dx],
                (mx, at_z(dz), my, mc),
            )
            copy.start()
            z_copies[dz, dx] = copy
        choose(x, mz, tgt_all.at[mz, x])

    row8 = rows_of((8, BLK))
    ones3 = jnp.where(row8 < 3, 1.0, 0.0)
    zeros = jnp.zeros((8, BLK), f32)

    for copy in s_copies:
        copy.wait_recv()

    def prepare_src(i, carry):
        v = unfold(src_all[i // OWN, pl.ds(pl.multiple_of(lax.rem(i, OWN) * 8, 8), 8), :])
        hi, mid, lo = split3(v)
        xx[i] = jnp.concatenate([hi, mid, hi, lo, hi, mid, ones3, zeros], axis=0).astype(bf16)
        src_w[i], src_w8[i] = sum_weights(v, row8)
        return carry

    lax.fori_loop(0, n_tgt * OWN, prepare_src, 0, unroll=2)

    def prepare_tgt(z, dx):
        x = lax.rem(mx + nx - dx, nx)
        for m in range(REQ):
            v = unfold(tgt_all[z, x, m])
            hi, mid, lo = split3(jnp.where(row8 < 3, SCALE * v, jnp.where(row8 == 3, 1.0, 0.0)))
            lhi, lmid, llo = split3(jnp.broadcast_to(v[3:4, :], (8, BLK)))
            level = jnp.where(
                row8 == 0, lhi, jnp.where(row8 == 1, lmid, jnp.where(row8 == 2, llo, 0.0))
            )
            i = (x * nz + z) * REQ + m
            yy[i] = jnp.concatenate([hi, hi, mid, hi, lo, mid, level, zeros], axis=0).astype(bf16)
            tgt_w[i], tgt_w8[i] = sum_weights(v, row8)

    for dz in [0] + far_first(nz)[::-1]:
        for dx in [0] + far_first(nx)[::-1]:
            if dz:
                z_copies[dz, dx].wait_recv()
            prepare_tgt(lax.rem(mz + nz - dz, nz), dx)

    b_copies = [
        send(
            own_req.at[lax.rem(at_r(d), nz), at_r(d) // nz],
            back_req.at[mr],
            b_send.at[d],
            b_recv.at[d],
            in_clus(at_r(d)),
        )
        for d in range(1, n_clus)
    ]
    for copy in b_copies:
        copy.start()
    back_req[mr] = own_req[mz, mx]

    top = rows_of((8, LANES)) < 4

    def fold(s, rest):
        s = s[:8] + s[8:] + rest[:8] * (1.0 / LO)
        return jnp.where(top, s[:, :LANES], pltpu.roll(s[:, LANES:], 4, 0))

    def exponent(k):
        return lax.dot_general(
            yy[pair_slot[k]],
            xx[pair_src[k]],
            (((0,), (0,)), ((), ())),
            preferred_element_type=f32,
        )

    def pair(k, expo):
        later = exponent(jnp.minimum(k + 1, pairs - 1))
        kern = jnp.exp2(expo)
        hi = kern.astype(bf16)
        lo = ((kern - hi.astype(f32)) * LO).astype(f8)
        j, i = pair_slot[k], pair_src[k]
        nt = (((1,), (1,)), ((), ()))
        s = fold(
            jnp.dot(tgt_w[j], hi, preferred_element_type=f32),
            jnp.dot(tgt_w8[j], lo, preferred_element_type=f32),
        )
        t = fold(
            lax.dot_general(src_w[i], hi, nt, preferred_element_type=f32),
            lax.dot_general(src_w8[i], lo, nt, preferred_element_type=f32),
        )
        src_parts[pl.ds(pl.multiple_of(k * 8, 8), 8), :] = s
        tgt_parts[pl.ds(pl.multiple_of(k * 8, 8), 8), :] = t
        return later

    lax.fori_loop(0, pairs, pair, exponent(0), unroll=16)

    def combine(names, count, parts, put):
        at = lax.broadcasted_iota(jnp.int32, (count, pairs), 1)
        pick = (jnp.broadcast_to(names[...], (count, pairs)) == rows_of((count, pairs))) & (
            at < jnp.broadcast_to(pair_count[...], (count, pairs))
        )
        pick = jnp.where(pick, 1.0, 0.0).astype(bf16)
        for r in range(8):
            parts_r = jnp.concatenate(split3(parts[pl.ds(r, pairs, stride=8), :]), axis=1)
            s = jnp.dot(pick, parts_r.astype(bf16), preferred_element_type=f32)
            put[pl.ds(r, count, stride=8), :] = (
                s[:, :LANES] + s[:, LANES : 2 * LANES] + s[:, 2 * LANES :]
            )

    combine(slot_row, slots, tgt_parts, tgt_send)

    def of_owner(ref, r):
        return ref.at[pl.ds(pl.multiple_of(r * (8 * REQ), 8 * REQ), 8 * REQ), :]

    t_copies = [
        send(
            of_owner(tgt_send, at_r(d)),
            tgt_back.at[mr],
            t_send.at[d],
            t_recv.at[d],
            in_clus(at_r(d)),
        )
        for d in range(1, n_clus)
    ]
    for copy in t_copies:
        copy.start()

    combine(src_row, n_tgt * OWN, src_parts, src_send)

    def of_group(ref, t):
        return ref.at[pl.ds(pl.multiple_of(t * (8 * OWN), 8 * OWN), 8 * OWN), :]

    r_copies = [
        send(
            of_group(src_send, at_t(d)),
            src_back.at[mt],
            r_send.at[d],
            r_recv.at[d],
            in_tgt(at_t(d)),
        )
        for d in range(1, n_tgt)
    ]
    for copy in r_copies:
        copy.start()
    tgt_back[mr] = of_owner(tgt_send, mr)[...]
    src_back[mt] = of_group(src_send, mt)[...]

    def finish(xs, weight_ref, pot_ref, live, out):
        us = get_tiles(total)
        comps = [xs[c] * us[3] - us[c] for c in range(3)]
        comps.append(pot_ref[...] - ENTROPIC * us[3] / weight_ref[...])
        put_tiles(out, [jnp.where(live, comp, 0.0) for comp in comps])

    for copy in b_copies + t_copies:
        copy.wait_recv()

    def add_tgt(r, sums):
        sums = list(sums)
        for m in range(REQ):
            which = jnp.broadcast_to(back_req[r, m : m + 1, :], (8, LANES))
            tile = tgt_back[r, m * 8 : m * 8 + 8, :]
            for b in range(OWN):
                sums[b] = sums[b] + jnp.where(which == b, tile, 0.0)
        return tuple(sums)

    sums = lax.fori_loop(0, n_clus, add_tgt, tuple(jnp.zeros((8, LANES), f32) for _ in range(OWN)))
    for b in range(OWN):
        total[b * 8 : b * 8 + 8, :] = sums[b]
    finish(txs, tgt_weight, tgt_pot, tlive, out_tgt)

    for copy in r_copies:
        copy.wait_recv()
    whole = src_back[0]
    for t in range(1, n_tgt):
        whole = whole + src_back[t]
    total[...] = whole
    finish(sxs, src_weight, src_pot, slive, out_src)

    for copy in (
        x_copies + q_copies + s_copies + list(z_copies.values()) + b_copies + t_copies + r_copies
    ):
        copy.wait_send()


def write_out(src, tgt, src_pos, src_weight, tgt_pos, tgt_weight):
    for tiles, pos, weight in ((src, src_pos, src_weight), (tgt, tgt_pos, tgt_weight)):
        for q in range(2 * OWN):
            pos[:, q * LANES : q * LANES + LANES] = tiles[q * 4 : q * 4 + 3, :]
        weight[...] = tiles[pl.ds(3, 2 * OWN, stride=4), :]


def shards(
    dims,
    src_pos,
    src_weight,
    src_pot,
    src_count,
    tgt_pos,
    tgt_weight,
    tgt_pot,
    tgt_count,
    requests,
    pair_src,
    pair_slot,
    pair_count,
):
    nx, nz, ny, nc = dims
    n_tgt, n_clus = ny * nc, nx * nz
    slots = n_clus * REQ
    pairs = pair_src.shape[0]
    quarters = 2 * OWN

    def tall(v):
        return v.reshape(*v.shape[:-1], quarters, LANES)

    vmem = pl.BlockSpec(memory_space=pltpu.VMEM)
    dma = pltpu.SemaphoreType.DMA
    inputs = [
        tgt_pos,
        tall(tgt_weight),
        tall(tgt_pot),
        tgt_count,
        requests.T,
        src_pos,
        tall(src_weight),
        tall(src_pot),
        src_count,
        pair_src,
        pair_slot,
        pair_count[None, :],
        pair_src[None, :],
        pair_slot[None, :],
    ]
    spaces = [pltpu.SMEM if i in (3, 4, 8, 9, 10) else pltpu.VMEM for i in range(14)]
    tiles = jax.ShapeDtypeStruct((8 * OWN, LANES), f32)
    sums = pl.pallas_call(
        functools.partial(kernel, dims),
        out_shape=[tiles, tiles],
        in_specs=[[pl.BlockSpec(memory_space=pltpu.HBM)] * len(inputs)],
        out_specs=[vmem] * 2,
        scratch_shapes=[
            [space(v.shape, v.dtype) for space, v in zip(spaces, inputs)],
            dma((len(inputs),)),
            pltpu.VMEM((n_tgt, 8 * OWN, LANES), f32),
            pltpu.VMEM((nx, 8 * OWN, LANES), f32),
            pltpu.VMEM((nz, nx, REQ, 8, LANES), f32),
            pltpu.VMEM((nz, nx, REQ, 8, LANES), f32),
            pltpu.VMEM((nz, nx, REQ, LANES), jnp.int32),
            pltpu.VMEM((nz, nx, REQ, LANES), jnp.int32),
            pltpu.VMEM((n_clus, REQ, LANES), jnp.int32),
            pltpu.VMEM((n_tgt * OWN, 64, BLK), bf16),
            pltpu.VMEM((slots, 64, BLK), bf16),
            pltpu.VMEM((n_tgt * OWN, 16, BLK), bf16),
            pltpu.VMEM((slots, 16, BLK), bf16),
            pltpu.VMEM((n_tgt * OWN, 32, BLK), f8),
            pltpu.VMEM((slots, 32, BLK), f8),
            pltpu.VMEM((pairs * 8, LANES), f32),
            pltpu.VMEM((pairs * 8, LANES), f32),
            pltpu.VMEM((n_tgt * OWN * 8, LANES), f32),
            pltpu.VMEM((slots * 8, LANES), f32),
            pltpu.VMEM((n_tgt, 8 * OWN, LANES), f32),
            pltpu.VMEM((n_clus, 8 * REQ, LANES), f32),
            pltpu.VMEM((8 * OWN, LANES), f32),
            dma((nx,)),
            dma((nx,)),
            dma((nz,)),
            dma((nz,)),
            dma((n_tgt,)),
            dma((n_tgt,)),
            dma((nz, nx)),
            dma((nz, nx)),
            dma((n_clus,)),
            dma((n_clus,)),
            dma((n_clus,)),
            dma((n_clus,)),
            dma((n_tgt,)),
            dma((n_tgt,)),
        ],
        compiler_params=pltpu.CompilerParams(
            collective_id=0, has_side_effects=True, vmem_limit_bytes=48 << 20
        ),
    )(
        [
            v if v.size == 1 else pltpu.with_memory_space_constraint(v, pltpu.HBM)
            for v in inputs
        ]
    )
    pos = jax.ShapeDtypeStruct((3, quarters * LANES), f32)
    weight = jax.ShapeDtypeStruct((quarters, LANES), f32)
    outs = pl.pallas_call(
        write_out,
        out_shape=[pos, weight, pos, weight],
        in_specs=[vmem] * 2,
        compiler_params=pltpu.CompilerParams(vmem_limit_bytes=4 << 20),
    )(*sums)
    return outs[0], outs[1].reshape(-1), outs[2], outs[3].reshape(-1)


def solution(mesh):
    n_clus, n_tgt = mesh.shape["clus"], mesh.shape["tgt"]
    nx = math.isqrt(n_clus)
    dims = (nx, n_clus // nx, n_tgt // 2, 2)
    torus = Mesh(mesh.devices.reshape(dims), AXES)
    wide, flat = P(None, AXES), P(AXES)
    return jax.shard_map(
        functools.partial(shards, dims),
        mesh=torus,
        in_specs=(
            wide,
            flat,
            flat,
            flat,
            wide,
            flat,
            flat,
            flat,
            P(AXES, None),
            flat,
            flat,
            flat,
        ),
        out_specs=(wide, flat, wide, flat),
        check_vma=False,
    )
```

```python
import functools
import math

import jax
import jax.numpy as jnp
from jax import lax
from jax.experimental import pallas as pl
from jax.experimental.pallas import tpu as pltpu
from jax.sharding import Mesh
from jax.sharding import PartitionSpec as P

AXES = ("x", "z", "y", "core")
MESH = pl.DeviceIdType.MESH
BLK = 256
LANES = 128
OWN = 8
REQ = 2
ENTROPIC = 0.05
SCALE = 1.0 / (ENTROPIC * math.log(2.0))
DEAD = -1.0e4
VMEM = 67043328
f32 = jnp.float32
bf16 = jnp.bfloat16
f8 = jnp.float8_e4m3fn
LO = 2.0**13


def far_first(n):
    return sorted(range(1, n), key=lambda d: (-min(d, n - d), d))


def others(n, m):
    near = [(min(i, n - i) + min(j, m - j), i, j) for i in range(n) for j in range(m)]
    return [(i, j) for _, i, j in sorted(near, key=lambda v: (-v[0], v[1:])) if i or j]


def split3(v):
    hi = v.astype(bf16).astype(f32)
    rest = v - hi
    mid = rest.astype(bf16).astype(f32)
    return hi, mid, rest - mid


def rows_of(shape):
    return lax.broadcasted_iota(jnp.int32, shape, 0)


def pack(pos_ref, weight_ref, pot_ref, count_ref):
    quarters = weight_ref.shape[0]
    row = rows_of((quarters, LANES))
    lane = lax.broadcasted_iota(jnp.int32, (quarters, LANES), 1)
    counts = jnp.zeros((quarters, LANES), jnp.int32)
    for b in range(OWN):
        counts = jnp.where((row >> 1) == b, count_ref[b], counts)
    live = ((row & 1) * LANES + lane) < counts
    xs = [
        jnp.concatenate(
            [pos_ref[c : c + 1, q * LANES : q * LANES + LANES] for q in range(quarters)], axis=0
        )
        - 0.5
        for c in range(3)
    ]
    square = xs[0] * xs[0] + xs[1] * xs[1] + xs[2] * xs[2]
    level = SCALE * (pot_ref[...] - 0.5 * square) + jnp.log(weight_ref[...]) * (1.0 / math.log(2.0))
    return xs, jnp.where(live, level, DEAD), live


def put_tiles(tiles, comps):
    for c, comp in enumerate(comps):
        tiles[pl.ds(c, 2 * OWN, stride=4), :] = comp


def get_tiles(tiles):
    return [tiles[pl.ds(c, 2 * OWN, stride=4), :] for c in range(4)]


def unfold(tile):
    return jnp.concatenate([tile, pltpu.roll(tile, 4, 0)], axis=1)


def sum_weights(v, row):
    w = jnp.where((row & 3) == 3, 1.0, v)
    hi = w.astype(bf16).astype(f32)
    coarse = jnp.concatenate([w, jnp.zeros((24, BLK), f32)], axis=0).astype(f8)
    return jnp.concatenate([hi, w - hi], axis=0).astype(bf16), coarse


def kernel(
    dims,
    inputs,
    out_src,
    out_tgt,
    held,
    in_sem,
    src_all,
    row_all,
    tgt_all,
    chosen,
    own_req,
    z_req,
    back_req,
    xx,
    yy,
    src_w,
    tgt_w,
    src_w8,
    tgt_w8,
    src_parts,
    tgt_parts,
    src_send,
    tgt_send,
    src_back,
    tgt_back,
    total,
    x_send,
    x_recv,
    q_send,
    q_recv,
    s_send,
    s_recv,
    z_send,
    z_recv,
    b_send,
    b_recv,
    t_send,
    t_recv,
    r_send,
    r_recv,
):
    nx, nz, ny, nc = dims
    n_tgt, n_clus = ny * nc, nx * nz
    slots = n_clus * REQ
    mx, mz, my, mc = (lax.axis_index(a) for a in AXES)
    mt, mr = my * nc + mc, mx * nz + mz

    def at_x(d):
        return lax.rem(mx + d, nx)

    def at_z(d):
        return lax.rem(mz + d, nz)

    def at_t(dy, dc):
        return lax.rem(my + dy, ny) * nc + lax.rem(mc + dc, nc)

    def at_r(dx, dz):
        return at_x(dx) * nz + at_z(dz)

    def in_tgt(dy, dc):
        return (mx, mz, lax.rem(my + dy, ny), lax.rem(mc + dc, nc))

    def in_clus(dx, dz):
        return (at_x(dx), at_z(dz), my, mc)

    tgt_peers = others(ny, nc)
    clus_peers = others(nx, nz)

    def send(src, dst, send_sem, recv_sem, device):
        return pltpu.make_async_remote_copy(
            src_ref=src,
            dst_ref=dst,
            send_sem=send_sem,
            recv_sem=recv_sem,
            device_id=device,
            device_id_type=MESH,
        )

    barrier = pltpu.get_barrier_semaphore()
    for d in range(1, nx):
        pl.semaphore_signal(barrier, inc=1, device_id=(at_x(d), mz, my, mc), device_id_type=MESH)
    for d in range(1, nz):
        pl.semaphore_signal(barrier, inc=1, device_id=(mx, at_z(d), my, mc), device_id_type=MESH)
    for d in tgt_peers:
        pl.semaphore_signal(barrier, inc=1, device_id=in_tgt(*d), device_id_type=MESH)

    loads = [
        pltpu.make_async_copy(src, dst, in_sem.at[i])
        for i, (src, dst) in enumerate(zip(inputs, held))
    ]
    for load in loads:
        load.start()
    (
        tgt_pos,
        tgt_weight,
        tgt_pot,
        tgt_count,
        requests,
        src_pos,
        src_weight,
        src_pot,
        src_count,
        pair_src,
        pair_slot,
        pair_count,
        src_row,
        slot_row,
    ) = held
    pairs = pair_src.shape[0]

    for load in loads[:5]:
        load.wait()
    txs, tlevel, tlive = pack(tgt_pos, tgt_weight, tgt_pot, tgt_count)
    put_tiles(row_all.at[mx], txs + [tlevel])
    for r in range(n_clus):
        for m in range(REQ):
            own_req[r % nz, r // nz, m] = jnp.full((LANES,), requests[m, r], jnp.int32)

    pl.semaphore_wait(barrier, nx - 1 + nz - 1 + n_tgt - 1)

    q_copies = [
        send(own_req.at[at_z(d)], z_req.at[mz], q_send.at[d], q_recv.at[d], (mx, at_z(d), my, mc))
        for d in far_first(nz)
    ]
    x_copies = [
        send(row_all.at[mx], row_all.at[mx], x_send.at[d], x_recv.at[d], (at_x(d), mz, my, mc))
        for d in far_first(nx)
    ]
    for copy in q_copies + x_copies:
        copy.start()
    z_req[mz] = own_req[mz]
    for load in loads[5:]:
        load.wait()
    sxs, slevel, slive = pack(src_pos, src_weight, src_pot, src_count)
    put_tiles(src_all.at[mt], sxs + [slevel])
    s_copies = [
        send(src_all.at[mt], src_all.at[mt], s_send.at[d], s_recv.at[d], in_tgt(*d))
        for d in tgt_peers
    ]
    for copy in s_copies:
        copy.start()

    def choose(x, asked, put):
        blocks = [row_all[x, b * 8 : b * 8 + 8, :] for b in range(OWN)]
        for m in range(REQ):
            which = jnp.broadcast_to(z_req[asked, x, m : m + 1, :], (8, LANES))
            tile = blocks[0]
            for b in range(1, OWN):
                tile = jnp.where(which == b, blocks[b], tile)
            put[m] = tile

    for copy in q_copies:
        copy.wait_recv()
    z_copies = {}
    for dx in [0] + far_first(nx)[::-1]:
        x = lax.rem(mx + nx - dx, nx)
        if dx:
            x_copies[far_first(nx).index(dx)].wait_recv()
        for dz in far_first(nz):
            choose(x, at_z(dz), chosen.at[dz, dx])
            copy = send(
                chosen.at[dz, dx],
                tgt_all.at[mz, x],
                z_send.at[dz, dx],
                z_recv.at[dz, dx],
                (mx, at_z(dz), my, mc),
            )
            copy.start()
            z_copies[dz, dx] = copy
        choose(x, mz, tgt_all.at[mz, x])

    row8 = rows_of((8, BLK))
    ones3 = jnp.where(row8 < 3, 1.0, 0.0)
    zeros = jnp.zeros((8, BLK), f32)

    for copy in s_copies:
        copy.wait_recv()

    def prepare_src(i, carry):
        v = unfold(src_all[i // OWN, pl.ds(pl.multiple_of(lax.rem(i, OWN) * 8, 8), 8), :])
        hi, mid, lo = split3(v)
        xx[i] = jnp.concatenate([hi, mid, hi, lo, hi, mid, ones3, zeros], axis=0).astype(bf16)
        src_w[i], src_w8[i] = sum_weights(v, row8)
        return carry

    lax.fori_loop(0, n_tgt * OWN, prepare_src, 0, unroll=2)

    def prepare_tgt(z, dx):
        x = lax.rem(mx + nx - dx, nx)
        for m in range(REQ):
            v = unfold(tgt_all[z, x, m])
            hi, mid, lo = split3(jnp.where(row8 < 3, SCALE * v, jnp.where(row8 == 3, 1.0, 0.0)))
            lhi, lmid, llo = split3(jnp.broadcast_to(v[3:4, :], (8, BLK)))
            level = jnp.where(
                row8 == 0, lhi, jnp.where(row8 == 1, lmid, jnp.where(row8 == 2, llo, 0.0))
            )
            i = (x * nz + z) * REQ + m
            yy[i] = jnp.concatenate([hi, hi, mid, hi, lo, mid, level, zeros], axis=0).astype(bf16)
            tgt_w[i], tgt_w8[i] = sum_weights(v, row8)

    for dz in [0] + far_first(nz)[::-1]:
        for dx in [0] + far_first(nx)[::-1]:
            if dz:
                z_copies[dz, dx].wait_recv()
            prepare_tgt(lax.rem(mz + nz - dz, nz), dx)

    b_copies = [
        send(
            own_req.at[at_z(d[1]), at_x(d[0])],
            back_req.at[mr],
            b_send.at[d],
            b_recv.at[d],
            in_clus(*d),
        )
        for d in clus_peers
    ]
    for copy in b_copies:
        copy.start()
    back_req[mr] = own_req[mz, mx]

    top = rows_of((8, LANES)) < 4

    def fold(s, rest):
        s = s[:8] + s[8:] + rest[:8] * (1.0 / LO)
        return jnp.where(top, s[:, :LANES], pltpu.roll(s[:, LANES:], 4, 0))

    def exponent(k):
        return lax.dot_general(
            yy[pair_slot[k]],
            xx[pair_src[k]],
            (((0,), (0,)), ((), ())),
            preferred_element_type=f32,
        )

    def pair(k, expo):
        later = exponent(jnp.minimum(k + 1, pairs - 1))
        kern = jnp.exp2(expo)
        hi = kern.astype(bf16)
        lo = ((kern - hi.astype(f32)) * LO).astype(f8)
        j, i = pair_slot[k], pair_src[k]
        nt = (((1,), (1,)), ((), ()))
        s = fold(
            jnp.dot(tgt_w[j], hi, preferred_element_type=f32),
            jnp.dot(tgt_w8[j], lo, preferred_element_type=f32),
        )
        t = fold(
            lax.dot_general(src_w[i], hi, nt, preferred_element_type=f32),
            lax.dot_general(src_w8[i], lo, nt, preferred_element_type=f32),
        )
        src_parts[pl.ds(pl.multiple_of(k * 8, 8), 8), :] = s
        tgt_parts[pl.ds(pl.multiple_of(k * 8, 8), 8), :] = t
        return later

    lax.fori_loop(0, pairs, pair, exponent(0), unroll=32)

    def combine(names, count, parts, put):
        at = lax.broadcasted_iota(jnp.int32, (count, pairs), 1)
        pick = (jnp.broadcast_to(names[...], (count, pairs)) == rows_of((count, pairs))) & (
            at < jnp.broadcast_to(pair_count[...], (count, pairs))
        )
        pick = jnp.where(pick, 1.0, 0.0).astype(bf16)
        for r in range(8):
            parts_r = jnp.concatenate(split3(parts[pl.ds(r, pairs, stride=8), :]), axis=1)
            s = jnp.dot(pick, parts_r.astype(bf16), preferred_element_type=f32)
            put[pl.ds(r, count, stride=8), :] = (
                s[:, :LANES] + s[:, LANES : 2 * LANES] + s[:, 2 * LANES :]
            )

    combine(slot_row, slots, tgt_parts, tgt_send)

    def of_owner(ref, r):
        return ref.at[pl.ds(pl.multiple_of(r * (8 * REQ), 8 * REQ), 8 * REQ), :]

    t_copies = [
        send(
            of_owner(tgt_send, at_r(*d)),
            tgt_back.at[mr],
            t_send.at[d],
            t_recv.at[d],
            in_clus(*d),
        )
        for d in clus_peers
    ]
    for copy in t_copies:
        copy.start()

    combine(src_row, n_tgt * OWN, src_parts, src_send)

    def of_group(ref, t):
        return ref.at[pl.ds(pl.multiple_of(t * (8 * OWN), 8 * OWN), 8 * OWN), :]

    r_copies = [
        send(
            of_group(src_send, at_t(*d)),
            src_back.at[mt],
            r_send.at[d],
            r_recv.at[d],
            in_tgt(*d),
        )
        for d in tgt_peers
    ]
    for copy in r_copies:
        copy.start()
    tgt_back[mr] = of_owner(tgt_send, mr)[...]
    src_back[mt] = of_group(src_send, mt)[...]

    def finish(xs, weight_ref, pot_ref, live, out):
        us = get_tiles(total)
        comps = [xs[c] * us[3] - us[c] for c in range(3)]
        comps.append(pot_ref[...] - ENTROPIC * us[3] / weight_ref[...])
        put_tiles(out, [jnp.where(live, comp, 0.0) for comp in comps])

    for copy in b_copies + t_copies:
        copy.wait_recv()

    def add_tgt(r, sums):
        sums = list(sums)
        for m in range(REQ):
            which = jnp.broadcast_to(back_req[r, m : m + 1, :], (8, LANES))
            tile = tgt_back[r, m * 8 : m * 8 + 8, :]
            for b in range(OWN):
                sums[b] = sums[b] + jnp.where(which == b, tile, 0.0)
        return tuple(sums)

    sums = lax.fori_loop(0, n_clus, add_tgt, tuple(jnp.zeros((8, LANES), f32) for _ in range(OWN)))
    for b in range(OWN):
        total[b * 8 : b * 8 + 8, :] = sums[b]
    finish(txs, tgt_weight, tgt_pot, tlive, out_tgt)

    for copy in r_copies:
        copy.wait_recv()
    whole = src_back[0]
    for t in range(1, n_tgt):
        whole = whole + src_back[t]
    total[...] = whole
    finish(sxs, src_weight, src_pot, slive, out_src)

    for copy in (
        x_copies + q_copies + s_copies + list(z_copies.values()) + b_copies + t_copies + r_copies
    ):
        copy.wait_send()


def write_out(src, tgt, src_pos, src_weight, tgt_pos, tgt_weight):
    for tiles, pos, weight in ((src, src_pos, src_weight), (tgt, tgt_pos, tgt_weight)):
        for q in range(2 * OWN):
            pos[:, q * LANES : q * LANES + LANES] = tiles[q * 4 : q * 4 + 3, :]
        weight[...] = tiles[pl.ds(3, 2 * OWN, stride=4), :]


def shards(
    dims,
    src_pos,
    src_weight,
    src_pot,
    src_count,
    tgt_pos,
    tgt_weight,
    tgt_pot,
    tgt_count,
    requests,
    pair_src,
    pair_slot,
    pair_count,
):
    nx, nz, ny, nc = dims
    n_tgt, n_clus = ny * nc, nx * nz
    slots = n_clus * REQ
    pairs = pair_src.shape[0]
    quarters = 2 * OWN

    def tall(v):
        return v.reshape(*v.shape[:-1], quarters, LANES)

    vmem = pl.BlockSpec(memory_space=pltpu.VMEM)
    dma = pltpu.SemaphoreType.DMA
    inputs = [
        tgt_pos,
        tall(tgt_weight),
        tall(tgt_pot),
        tgt_count,
        requests.T,
        src_pos,
        tall(src_weight),
        tall(src_pot),
        src_count,
        pair_src,
        pair_slot,
        pair_count[None, :],
        pair_src[None, :],
        pair_slot[None, :],
    ]
    spaces = [pltpu.SMEM if i in (3, 4, 8, 9, 10) else pltpu.VMEM for i in range(14)]
    tiles = jax.ShapeDtypeStruct((8 * OWN, LANES), f32)
    sums = pl.pallas_call(
        functools.partial(kernel, dims),
        out_shape=[tiles, tiles],
        in_specs=[[pl.BlockSpec(memory_space=pltpu.HBM)] * len(inputs)],
        out_specs=[vmem] * 2,
        scratch_shapes=[
            [space(v.shape, v.dtype) for space, v in zip(spaces, inputs)],
            dma((len(inputs),)),
            pltpu.VMEM((n_tgt, 8 * OWN, LANES), f32),
            pltpu.VMEM((nx, 8 * OWN, LANES), f32),
            pltpu.VMEM((nz, nx, REQ, 8, LANES), f32),
            pltpu.VMEM((nz, nx, REQ, 8, LANES), f32),
            pltpu.VMEM((nz, nx, REQ, LANES), jnp.int32),
            pltpu.VMEM((nz, nx, REQ, LANES), jnp.int32),
            pltpu.VMEM((n_clus, REQ, LANES), jnp.int32),
            pltpu.VMEM((n_tgt * OWN, 64, BLK), bf16),
            pltpu.VMEM((slots, 64, BLK), bf16),
            pltpu.VMEM((n_tgt * OWN, 16, BLK), bf16),
            pltpu.VMEM((slots, 16, BLK), bf16),
            pltpu.VMEM((n_tgt * OWN, 32, BLK), f8),
            pltpu.VMEM((slots, 32, BLK), f8),
            pltpu.VMEM((pairs * 8, LANES), f32),
            pltpu.VMEM((pairs * 8, LANES), f32),
            pltpu.VMEM((n_tgt * OWN * 8, LANES), f32),
            pltpu.VMEM((slots * 8, LANES), f32),
            pltpu.VMEM((n_tgt, 8 * OWN, LANES), f32),
            pltpu.VMEM((n_clus, 8 * REQ, LANES), f32),
            pltpu.VMEM((8 * OWN, LANES), f32),
            dma((nx,)),
            dma((nx,)),
            dma((nz,)),
            dma((nz,)),
            dma((ny, nc)),
            dma((ny, nc)),
            dma((nz, nx)),
            dma((nz, nx)),
            dma((nx, nz)),
            dma((nx, nz)),
            dma((nx, nz)),
            dma((nx, nz)),
            dma((ny, nc)),
            dma((ny, nc)),
        ],
        compiler_params=pltpu.CompilerParams(
            collective_id=0, has_side_effects=True, vmem_limit_bytes=48 << 20
        ),
    )(
        [
            v if v.size == 1 else pltpu.with_memory_space_constraint(v, pltpu.HBM)
            for v in inputs
        ]
    )
    pos = jax.ShapeDtypeStruct((3, quarters * LANES), f32)
    weight = jax.ShapeDtypeStruct((quarters, LANES), f32)
    outs = pl.pallas_call(
        write_out,
        out_shape=[pos, weight, pos, weight],
        in_specs=[vmem] * 2,
        compiler_params=pltpu.CompilerParams(vmem_limit_bytes=4 << 20),
    )(*sums)
    return outs[0], outs[1].reshape(-1), outs[2], outs[3].reshape(-1)


def solution(mesh):
    n_clus, n_tgt = mesh.shape["clus"], mesh.shape["tgt"]
    nx = math.isqrt(n_clus)
    dims = (nx, n_clus // nx, n_tgt // 2, 2)
    torus = Mesh(mesh.devices.reshape(dims), AXES)
    wide, flat = P(None, AXES), P(AXES)
    return jax.shard_map(
        functools.partial(shards, dims),
        mesh=torus,
        in_specs=(
            wide,
            flat,
            flat,
            flat,
            wide,
            flat,
            flat,
            flat,
            P(AXES, None),
            flat,
            flat,
            flat,
        ),
        out_specs=(wide, flat, wide, flat),
        check_vma=False,
    )
```

```python
import functools
import math

import jax
import jax.numpy as jnp
from jax import lax
from jax.experimental import pallas as pl
from jax.experimental.pallas import tpu as pltpu
from jax.sharding import Mesh
from jax.sharding import PartitionSpec as P

AXES = ("x", "z", "y", "core")
MESH = pl.DeviceIdType.MESH
BLK = 256
LANES = 128
OWN = 8
REQ = 2
ENTROPIC = 0.05
SCALE = 1.0 / (ENTROPIC * math.log(2.0))
DEAD = -1.0e4
VMEM = 67043328
f32 = jnp.float32
bf16 = jnp.bfloat16
f8 = jnp.float8_e4m3fn
LO = 2.0**13


def far_first(n):
    return sorted(range(1, n), key=lambda d: (-min(d, n - d), d))


def others(n, m):
    near = [(min(i, n - i) + min(j, m - j), i, j) for i in range(n) for j in range(m)]
    return [(i, j) for _, i, j in sorted(near, key=lambda v: (-v[0], v[1:])) if i or j]


def split3(v):
    hi = v.astype(bf16).astype(f32)
    rest = v - hi
    mid = rest.astype(bf16).astype(f32)
    return hi, mid, rest - mid


def rows_of(shape):
    return lax.broadcasted_iota(jnp.int32, shape, 0)


def pack(pos_ref, weight_ref, pot_ref, count_ref):
    quarters = weight_ref.shape[0]
    row = rows_of((quarters, LANES))
    lane = lax.broadcasted_iota(jnp.int32, (quarters, LANES), 1)
    counts = jnp.zeros((quarters, LANES), jnp.int32)
    for b in range(OWN):
        counts = jnp.where((row >> 1) == b, count_ref[b], counts)
    live = ((row & 1) * LANES + lane) < counts
    xs = [
        jnp.concatenate(
            [pos_ref[c : c + 1, q * LANES : q * LANES + LANES] for q in range(quarters)], axis=0
        )
        - 0.5
        for c in range(3)
    ]
    square = xs[0] * xs[0] + xs[1] * xs[1] + xs[2] * xs[2]
    level = SCALE * (pot_ref[...] - 0.5 * square) + jnp.log(weight_ref[...]) * (1.0 / math.log(2.0))
    return xs, jnp.where(live, level, DEAD), live


def put_tiles(tiles, comps):
    for c, comp in enumerate(comps):
        tiles[pl.ds(c, 2 * OWN, stride=4), :] = comp


def get_tiles(tiles):
    return [tiles[pl.ds(c, 2 * OWN, stride=4), :] for c in range(4)]


def unfold(tile):
    return jnp.concatenate([tile, pltpu.roll(tile, 4, 0)], axis=1)


def sum_weights(v, row):
    w = jnp.where((row & 3) == 3, 1.0, v)
    hi = w.astype(bf16).astype(f32)
    coarse = jnp.concatenate([w, jnp.zeros((24, BLK), f32)], axis=0).astype(f8)
    return jnp.concatenate([hi, w - hi], axis=0).astype(bf16), coarse


def kernel(
    dims,
    inputs,
    out_src,
    out_tgt,
    held,
    in_sem,
    src_order,
    slot_order,
    pair_src,
    pair_slot,
    order_sem,
    src_all,
    row_all,
    tgt_all,
    chosen,
    own_req,
    z_req,
    back_req,
    xx,
    yy,
    src_w,
    tgt_w,
    src_w8,
    tgt_w8,
    src_parts,
    tgt_parts,
    src_send,
    tgt_send,
    src_back,
    tgt_back,
    total,
    x_send,
    x_recv,
    q_send,
    q_recv,
    s_send,
    s_recv,
    z_send,
    z_recv,
    b_send,
    b_recv,
    t_send,
    t_recv,
    r_send,
    r_recv,
):
    nx, nz, ny, nc = dims
    n_tgt, n_clus = ny * nc, nx * nz
    slots = n_clus * REQ
    mx, mz, my, mc = (lax.axis_index(a) for a in AXES)
    mt, mr = my * nc + mc, mx * nz + mz

    def at_x(d):
        return lax.rem(mx + d, nx)

    def at_z(d):
        return lax.rem(mz + d, nz)

    def at_t(dy, dc):
        return lax.rem(my + dy, ny) * nc + lax.rem(mc + dc, nc)

    def at_r(dx, dz):
        return at_x(dx) * nz + at_z(dz)

    def in_tgt(dy, dc):
        return (mx, mz, lax.rem(my + dy, ny), lax.rem(mc + dc, nc))

    def in_clus(dx, dz):
        return (at_x(dx), at_z(dz), my, mc)

    tgt_peers = others(ny, nc)
    clus_peers = others(nx, nz)

    def send(src, dst, send_sem, recv_sem, device):
        return pltpu.make_async_remote_copy(
            src_ref=src,
            dst_ref=dst,
            send_sem=send_sem,
            recv_sem=recv_sem,
            device_id=device,
            device_id_type=MESH,
        )

    barrier = pltpu.get_barrier_semaphore()
    for d in range(1, nx):
        pl.semaphore_signal(barrier, inc=1, device_id=(at_x(d), mz, my, mc), device_id_type=MESH)
    for d in range(1, nz):
        pl.semaphore_signal(barrier, inc=1, device_id=(mx, at_z(d), my, mc), device_id_type=MESH)
    for d in tgt_peers:
        pl.semaphore_signal(barrier, inc=1, device_id=in_tgt(*d), device_id_type=MESH)

    loads = [
        pltpu.make_async_copy(src, dst, in_sem.at[i])
        for i, (src, dst) in enumerate(zip(inputs, held))
    ]
    for load in loads:
        load.start()
    (
        tgt_pos,
        tgt_weight,
        tgt_pot,
        tgt_count,
        requests,
        src_pos,
        src_weight,
        src_pot,
        src_count,
        pair_count,
        src_row,
        slot_row,
    ) = held
    pairs = src_row.shape[1]

    for load in loads[:5]:
        load.wait()
    txs, tlevel, tlive = pack(tgt_pos, tgt_weight, tgt_pot, tgt_count)
    put_tiles(row_all.at[mx], txs + [tlevel])
    for r in range(n_clus):
        for m in range(REQ):
            own_req[r % nz, r // nz, m] = jnp.full((LANES,), requests[m, r], jnp.int32)

    pl.semaphore_wait(barrier, nx - 1 + nz - 1 + n_tgt - 1)

    q_copies = [
        send(own_req.at[at_z(d)], z_req.at[mz], q_send.at[d], q_recv.at[d], (mx, at_z(d), my, mc))
        for d in far_first(nz)
    ]
    x_copies = [
        send(row_all.at[mx], row_all.at[mx], x_send.at[d], x_recv.at[d], (at_x(d), mz, my, mc))
        for d in far_first(nx)
    ]
    for copy in q_copies + x_copies:
        copy.start()
    z_req[mz] = own_req[mz]
    for load in loads[5:]:
        load.wait()
    sxs, slevel, slive = pack(src_pos, src_weight, src_pot, src_count)
    put_tiles(src_all.at[mt], sxs + [slevel])
    s_copies = [
        send(src_all.at[mt], src_all.at[mt], s_send.at[d], s_recv.at[d], in_tgt(*d))
        for d in tgt_peers
    ]
    for copy in s_copies:
        copy.start()

    xs_near, zs_near = [0] + far_first(nx)[::-1], [0] + far_first(nz)[::-1]
    square = (pairs, pairs)
    down = rows_of(square)
    across = lax.broadcasted_iota(jnp.int32, square, 1)

    def column(v):
        v = jnp.where(down == across, jnp.broadcast_to(v, square), 0)
        return jnp.broadcast_to(jnp.sum(v, axis=1, keepdims=True), square)

    slot = slot_row[...]
    owner = slot >> 1
    behind_x = (mx - (owner >> (nz.bit_length() - 1))) & (nx - 1)
    behind_z = (mz - owner) & (nz - 1)
    place = slot & 1
    for i, d in enumerate(xs_near):
        place = place + jnp.where(behind_x == d, i * REQ, 0)
    for i, d in enumerate(zs_near):
        place = place + jnp.where(behind_z == d, i * nx * REQ, 0)
    dead = lax.broadcasted_iota(jnp.int32, (1, pairs), 1) >= pair_count[...]
    place = jnp.where(dead, 2 * pairs, place)
    theirs, mine = jnp.broadcast_to(place, square), column(place)
    before = (theirs < mine) | ((theirs == mine) & (across < down))
    rank = jnp.sum(jnp.where(before, 1, 0), axis=1, keepdims=True)
    hit = jnp.broadcast_to(rank, square) == across
    orders = []
    for i, (row, order, scalars) in enumerate(
        ((src_row, src_order, pair_src), (slot_row, slot_order, pair_slot))
    ):
        values = jnp.where(hit, column(row[...]), 0)
        order[...] = jnp.sum(values, axis=0, keepdims=True)
        orders.append(pltpu.make_async_copy(order, scalars, order_sem.at[i]))
        orders[-1].start()

    def choose(x, asked, put):
        blocks = [row_all[x, b * 8 : b * 8 + 8, :] for b in range(OWN)]
        for m in range(REQ):
            which = jnp.broadcast_to(z_req[asked, x, m : m + 1, :], (8, LANES))
            tile = blocks[0]
            for b in range(1, OWN):
                tile = jnp.where(which == b, blocks[b], tile)
            put[m] = tile

    for copy in q_copies:
        copy.wait_recv()
    z_copies = {}
    for dx in xs_near:
        x = lax.rem(mx + nx - dx, nx)
        if dx:
            x_copies[far_first(nx).index(dx)].wait_recv()
        for dz in far_first(nz):
            choose(x, at_z(dz), chosen.at[dz, dx])
            copy = send(
                chosen.at[dz, dx],
                tgt_all.at[mz, x],
                z_send.at[dz, dx],
                z_recv.at[dz, dx],
                (mx, at_z(dz), my, mc),
            )
            copy.start()
            z_copies[dz, dx] = copy
        choose(x, mz, tgt_all.at[mz, x])

    row8 = rows_of((8, BLK))
    ones3 = jnp.where(row8 < 3, 1.0, 0.0)
    zeros = jnp.zeros((8, BLK), f32)

    def prepare_tgt(z, dx):
        x = lax.rem(mx + nx - dx, nx)
        for m in range(REQ):
            v = unfold(tgt_all[z, x, m])
            hi, mid, lo = split3(jnp.where(row8 < 3, SCALE * v, jnp.where(row8 == 3, 1.0, 0.0)))
            lhi, lmid, llo = split3(jnp.broadcast_to(v[3:4, :], (8, BLK)))
            level = jnp.where(
                row8 == 0, lhi, jnp.where(row8 == 1, lmid, jnp.where(row8 == 2, llo, 0.0))
            )
            i = (x * nz + z) * REQ + m
            yy[i] = jnp.concatenate([hi, hi, mid, hi, lo, mid, level, zeros], axis=0).astype(bf16)
            tgt_w[i], tgt_w8[i] = sum_weights(v, row8)

    top = rows_of((8, LANES)) < 4

    def fold(s, rest):
        s = s[:8] + s[8:] + rest[:8] * (1.0 / LO)
        return jnp.where(top, s[:, :LANES], pltpu.roll(s[:, LANES:], 4, 0))

    def exponent(k):
        return lax.dot_general(
            yy[pair_slot[0, k]],
            xx[pair_src[0, k]],
            (((0,), (0,)), ((), ())),
            preferred_element_type=f32,
        )

    def pair(last, k, expo):
        later = exponent(jnp.minimum(k + 1, last))
        kern = jnp.exp2(expo)
        hi = kern.astype(bf16)
        lo = ((kern - hi.astype(f32)) * LO).astype(f8)
        j, i = pair_slot[0, k], pair_src[0, k]
        nt = (((1,), (1,)), ((), ()))
        s = fold(
            jnp.dot(tgt_w[j], hi, preferred_element_type=f32),
            jnp.dot(tgt_w8[j], lo, preferred_element_type=f32),
        )
        t = fold(
            lax.dot_general(src_w[i], hi, nt, preferred_element_type=f32),
            lax.dot_general(src_w8[i], lo, nt, preferred_element_type=f32),
        )
        src_parts[pl.ds(pl.multiple_of(k * 8, 8), 8), :] = s
        tgt_parts[pl.ds(pl.multiple_of(k * 8, 8), 8), :] = t
        return later

    def run(first, end):
        unroll = next(u for u in range(min(end - first, 24), 0, -1) if (end - first) % u == 0)
        lax.fori_loop(
            first, end, functools.partial(pair, end - 1), exponent(first), unroll=unroll
        )

    def arrive(dzs):
        for dz in dzs:
            for dx in xs_near:
                if dz:
                    z_copies[dz, dx].wait_recv()
                prepare_tgt(lax.rem(mz + nz - dz, nz), dx)

    arrive(zs_near[:1])
    for copy in s_copies:
        copy.wait_recv()

    def prepare_src(i, carry):
        v = unfold(src_all[i // OWN, pl.ds(pl.multiple_of(lax.rem(i, OWN) * 8, 8), 8), :])
        hi, mid, lo = split3(v)
        xx[i] = jnp.concatenate([hi, mid, hi, lo, hi, mid, ones3, zeros], axis=0).astype(bf16)
        src_w[i], src_w8[i] = sum_weights(v, row8)
        return carry

    lax.fori_loop(0, n_tgt * OWN, prepare_src, 0, unroll=2)

    for copy in orders:
        copy.wait()
    row_slots = nx * REQ
    run(0, row_slots)
    if nz > 2:
        arrive(zs_near[1:-1])
        run(row_slots, (nz - 1) * row_slots)
    arrive(zs_near[-1:])

    b_copies = [
        send(
            own_req.at[at_z(d[1]), at_x(d[0])],
            back_req.at[mr],
            b_send.at[d],
            b_recv.at[d],
            in_clus(*d),
        )
        for d in clus_peers
    ]
    for copy in b_copies:
        copy.start()
    back_req[mr] = own_req[mz, mx]

    run(max(nz - 1, 1) * row_slots, pairs)

    def combine(names, count, parts, put):
        at = lax.broadcasted_iota(jnp.int32, (count, pairs), 1)
        pick = (jnp.broadcast_to(names[...], (count, pairs)) == rows_of((count, pairs))) & (
            at < jnp.broadcast_to(pair_count[...], (count, pairs))
        )
        pick = jnp.where(pick, 1.0, 0.0).astype(bf16)
        for r in range(8):
            parts_r = jnp.concatenate(split3(parts[pl.ds(r, pairs, stride=8), :]), axis=1)
            s = jnp.dot(pick, parts_r.astype(bf16), preferred_element_type=f32)
            put[pl.ds(r, count, stride=8), :] = (
                s[:, :LANES] + s[:, LANES : 2 * LANES] + s[:, 2 * LANES :]
            )

    combine(slot_order, slots, tgt_parts, tgt_send)

    def of_owner(ref, r):
        return ref.at[pl.ds(pl.multiple_of(r * (8 * REQ), 8 * REQ), 8 * REQ), :]

    t_copies = [
        send(
            of_owner(tgt_send, at_r(*d)),
            tgt_back.at[mr],
            t_send.at[d],
            t_recv.at[d],
            in_clus(*d),
        )
        for d in clus_peers
    ]
    for copy in t_copies:
        copy.start()

    combine(src_order, n_tgt * OWN, src_parts, src_send)

    def of_group(ref, t):
        return ref.at[pl.ds(pl.multiple_of(t * (8 * OWN), 8 * OWN), 8 * OWN), :]

    r_copies = [
        send(
            of_group(src_send, at_t(*d)),
            src_back.at[mt],
            r_send.at[d],
            r_recv.at[d],
            in_tgt(*d),
        )
        for d in tgt_peers
    ]
    for copy in r_copies:
        copy.start()
    tgt_back[mr] = of_owner(tgt_send, mr)[...]
    src_back[mt] = of_group(src_send, mt)[...]

    def finish(xs, weight_ref, pot_ref, live, out):
        us = get_tiles(total)
        comps = [xs[c] * us[3] - us[c] for c in range(3)]
        comps.append(pot_ref[...] - ENTROPIC * us[3] / weight_ref[...])
        put_tiles(out, [jnp.where(live, comp, 0.0) for comp in comps])

    for copy in b_copies + t_copies:
        copy.wait_recv()

    def add_tgt(r, sums):
        sums = list(sums)
        for m in range(REQ):
            which = jnp.broadcast_to(back_req[r, m : m + 1, :], (8, LANES))
            tile = tgt_back[r, m * 8 : m * 8 + 8, :]
            for b in range(OWN):
                sums[b] = sums[b] + jnp.where(which == b, tile, 0.0)
        return tuple(sums)

    sums = lax.fori_loop(0, n_clus, add_tgt, tuple(jnp.zeros((8, LANES), f32) for _ in range(OWN)))
    for b in range(OWN):
        total[b * 8 : b * 8 + 8, :] = sums[b]
    finish(txs, tgt_weight, tgt_pot, tlive, out_tgt)

    for copy in r_copies:
        copy.wait_recv()
    whole = src_back[0]
    for t in range(1, n_tgt):
        whole = whole + src_back[t]
    total[...] = whole
    finish(sxs, src_weight, src_pot, slive, out_src)

    for copy in (
        x_copies + q_copies + s_copies + list(z_copies.values()) + b_copies + t_copies + r_copies
    ):
        copy.wait_send()


def write_out(src, tgt, src_pos, src_weight, tgt_pos, tgt_weight):
    for tiles, pos, weight in ((src, src_pos, src_weight), (tgt, tgt_pos, tgt_weight)):
        for q in range(2 * OWN):
            pos[:, q * LANES : q * LANES + LANES] = tiles[q * 4 : q * 4 + 3, :]
        weight[...] = tiles[pl.ds(3, 2 * OWN, stride=4), :]


def shards(
    dims,
    src_pos,
    src_weight,
    src_pot,
    src_count,
    tgt_pos,
    tgt_weight,
    tgt_pot,
    tgt_count,
    requests,
    pair_src,
    pair_slot,
    pair_count,
):
    nx, nz, ny, nc = dims
    n_tgt, n_clus = ny * nc, nx * nz
    slots = n_clus * REQ
    pairs = pair_src.shape[0]
    quarters = 2 * OWN

    def tall(v):
        return v.reshape(*v.shape[:-1], quarters, LANES)

    vmem = pl.BlockSpec(memory_space=pltpu.VMEM)
    dma = pltpu.SemaphoreType.DMA
    inputs = [
        tgt_pos,
        tall(tgt_weight),
        tall(tgt_pot),
        tgt_count,
        requests.T,
        src_pos,
        tall(src_weight),
        tall(src_pot),
        src_count,
        pair_count[None, :],
        pair_src[None, :],
        pair_slot[None, :],
    ]
    spaces = [pltpu.SMEM if i in (3, 4, 8) else pltpu.VMEM for i in range(12)]
    tiles = jax.ShapeDtypeStruct((8 * OWN, LANES), f32)
    sums = pl.pallas_call(
        functools.partial(kernel, dims),
        out_shape=[tiles, tiles],
        in_specs=[[pl.BlockSpec(memory_space=pltpu.HBM)] * len(inputs)],
        out_specs=[vmem] * 2,
        scratch_shapes=[
            [space(v.shape, v.dtype) for space, v in zip(spaces, inputs)],
            dma((len(inputs),)),
            pltpu.VMEM((1, pairs), jnp.int32),
            pltpu.VMEM((1, pairs), jnp.int32),
            pltpu.SMEM((1, pairs), jnp.int32),
            pltpu.SMEM((1, pairs), jnp.int32),
            dma((2,)),
            pltpu.VMEM((n_tgt, 8 * OWN, LANES), f32),
            pltpu.VMEM((nx, 8 * OWN, LANES), f32),
            pltpu.VMEM((nz, nx, REQ, 8, LANES), f32),
            pltpu.VMEM((nz, nx, REQ, 8, LANES), f32),
            pltpu.VMEM((nz, nx, REQ, LANES), jnp.int32),
            pltpu.VMEM((nz, nx, REQ, LANES), jnp.int32),
            pltpu.VMEM((n_clus, REQ, LANES), jnp.int32),
            pltpu.VMEM((n_tgt * OWN, 64, BLK), bf16),
            pltpu.VMEM((slots, 64, BLK), bf16),
            pltpu.VMEM((n_tgt * OWN, 16, BLK), bf16),
            pltpu.VMEM((slots, 16, BLK), bf16),
            pltpu.VMEM((n_tgt * OWN, 32, BLK), f8),
            pltpu.VMEM((slots, 32, BLK), f8),
            pltpu.VMEM((pairs * 8, LANES), f32),
            pltpu.VMEM((pairs * 8, LANES), f32),
            pltpu.VMEM((n_tgt * OWN * 8, LANES), f32),
            pltpu.VMEM((slots * 8, LANES), f32),
            pltpu.VMEM((n_tgt, 8 * OWN, LANES), f32),
            pltpu.VMEM((n_clus, 8 * REQ, LANES), f32),
            pltpu.VMEM((8 * OWN, LANES), f32),
            dma((nx,)),
            dma((nx,)),
            dma((nz,)),
            dma((nz,)),
            dma((ny, nc)),
            dma((ny, nc)),
            dma((nz, nx)),
            dma((nz, nx)),
            dma((nx, nz)),
            dma((nx, nz)),
            dma((nx, nz)),
            dma((nx, nz)),
            dma((ny, nc)),
            dma((ny, nc)),
        ],
        compiler_params=pltpu.CompilerParams(
            collective_id=0, has_side_effects=True, vmem_limit_bytes=48 << 20
        ),
    )(
        [
            v if v.size == 1 else pltpu.with_memory_space_constraint(v, pltpu.HBM)
            for v in inputs
        ]
    )
    pos = jax.ShapeDtypeStruct((3, quarters * LANES), f32)
    weight = jax.ShapeDtypeStruct((quarters, LANES), f32)
    outs = pl.pallas_call(
        write_out,
        out_shape=[pos, weight, pos, weight],
        in_specs=[vmem] * 2,
        compiler_params=pltpu.CompilerParams(vmem_limit_bytes=4 << 20),
    )(*sums)
    return outs[0], outs[1].reshape(-1), outs[2], outs[3].reshape(-1)


def solution(mesh):
    n_clus, n_tgt = mesh.shape["clus"], mesh.shape["tgt"]
    nx = math.isqrt(n_clus)
    dims = (nx, n_clus // nx, n_tgt // 2, 2)
    torus = Mesh(mesh.devices.reshape(dims), AXES)
    wide, flat = P(None, AXES), P(AXES)
    return jax.shard_map(
        functools.partial(shards, dims),
        mesh=torus,
        in_specs=(
            wide,
            flat,
            flat,
            flat,
            wide,
            flat,
            flat,
            flat,
            P(AXES, None),
            flat,
            flat,
            flat,
        ),
        out_specs=(wide, flat, wide, flat),
        check_vma=False,
    )
```

```python
import functools
import math

import jax
import jax.numpy as jnp
from jax import lax
from jax.experimental import pallas as pl
from jax.experimental.pallas import tpu as pltpu
from jax.sharding import Mesh
from jax.sharding import PartitionSpec as P

AXES = ("x", "z", "y", "core")
MESH = pl.DeviceIdType.MESH
BLK = 256
LANES = 128
OWN = 8
REQ = 2
ENTROPIC = 0.05
SCALE = 1.0 / (ENTROPIC * math.log(2.0))
DEAD = -1.0e4
VMEM = 67043328
f32 = jnp.float32
bf16 = jnp.bfloat16
f8 = jnp.float8_e4m3fn
LO = 2.0**13


def far_first(n):
    return sorted(range(1, n), key=lambda d: (-min(d, n - d), d))


def others(n, m):
    near = [(min(i, n - i) + min(j, m - j), i, j) for i in range(n) for j in range(m)]
    return [(i, j) for _, i, j in sorted(near, key=lambda v: (-v[0], v[1:])) if i or j]


def split3(v):
    hi = v.astype(bf16).astype(f32)
    rest = v - hi
    mid = rest.astype(bf16).astype(f32)
    return hi, mid, rest - mid


def rows_of(shape):
    return lax.broadcasted_iota(jnp.int32, shape, 0)


def pack(pos_ref, weight_ref, pot_ref, count_ref):
    quarters = weight_ref.shape[0]
    row = rows_of((quarters, LANES))
    lane = lax.broadcasted_iota(jnp.int32, (quarters, LANES), 1)
    counts = jnp.zeros((quarters, LANES), jnp.int32)
    for b in range(OWN):
        counts = jnp.where((row >> 1) == b, count_ref[b], counts)
    live = ((row & 1) * LANES + lane) < counts
    xs = [
        jnp.concatenate(
            [pos_ref[c : c + 1, q * LANES : q * LANES + LANES] for q in range(quarters)], axis=0
        )
        - 0.5
        for c in range(3)
    ]
    square = xs[0] * xs[0] + xs[1] * xs[1] + xs[2] * xs[2]
    level = SCALE * (pot_ref[...] - 0.5 * square) + jnp.log(weight_ref[...]) * (1.0 / math.log(2.0))
    return xs, jnp.where(live, level, DEAD), live


def put_tiles(tiles, comps):
    for c, comp in enumerate(comps):
        tiles[pl.ds(c, 2 * OWN, stride=4), :] = comp


def get_tiles(tiles):
    return [tiles[pl.ds(c, 2 * OWN, stride=4), :] for c in range(4)]


def unfold(tile):
    return jnp.concatenate([tile, pltpu.roll(tile, 4, 0)], axis=1)


def sum_weights(v, row):
    w = jnp.where((row & 3) == 3, 1.0, v)
    hi = w.astype(bf16).astype(f32)
    coarse = jnp.concatenate([w, jnp.zeros((24, BLK), f32)], axis=0).astype(f8)
    return jnp.concatenate([hi, w - hi], axis=0).astype(bf16), coarse


def kernel(
    dims,
    inputs,
    out_src,
    out_tgt,
    held,
    in_sem,
    src_order,
    slot_order,
    pair_src,
    pair_slot,
    order_sem,
    src_all,
    row_all,
    tgt_all,
    chosen,
    own_req,
    z_req,
    back_req,
    xx,
    yy,
    src_w,
    tgt_w,
    src_w8,
    tgt_w8,
    src_parts,
    tgt_parts,
    src_send,
    tgt_send,
    src_back,
    tgt_back,
    total,
    x_send,
    x_recv,
    q_send,
    q_recv,
    s_send,
    s_recv,
    z_send,
    z_recv,
    b_send,
    b_recv,
    t_send,
    t_recv,
    r_send,
    r_recv,
):
    nx, nz, ny, nc = dims
    n_tgt, n_clus = ny * nc, nx * nz
    slots = n_clus * REQ
    mx, mz, my, mc = (lax.axis_index(a) for a in AXES)
    mt, mr = my * nc + mc, mx * nz + mz

    def at_x(d):
        return lax.rem(mx + d, nx)

    def at_z(d):
        return lax.rem(mz + d, nz)

    def at_t(dy, dc):
        return lax.rem(my + dy, ny) * nc + lax.rem(mc + dc, nc)

    def at_r(dx, dz):
        return at_x(dx) * nz + at_z(dz)

    def in_tgt(dy, dc):
        return (mx, mz, lax.rem(my + dy, ny), lax.rem(mc + dc, nc))

    def in_clus(dx, dz):
        return (at_x(dx), at_z(dz), my, mc)

    tgt_peers = others(ny, nc)
    clus_peers = others(nx, nz)

    def send(src, dst, send_sem, recv_sem, device):
        return pltpu.make_async_remote_copy(
            src_ref=src,
            dst_ref=dst,
            send_sem=send_sem,
            recv_sem=recv_sem,
            device_id=device,
            device_id_type=MESH,
        )

    barrier = pltpu.get_barrier_semaphore()
    for d in range(1, nx):
        pl.semaphore_signal(barrier, inc=1, device_id=(at_x(d), mz, my, mc), device_id_type=MESH)
    for d in range(1, nz):
        pl.semaphore_signal(barrier, inc=1, device_id=(mx, at_z(d), my, mc), device_id_type=MESH)
    for d in tgt_peers:
        pl.semaphore_signal(barrier, inc=1, device_id=in_tgt(*d), device_id_type=MESH)

    loads = [
        pltpu.make_async_copy(src, dst, in_sem.at[i])
        for i, (src, dst) in enumerate(zip(inputs, held))
    ]
    for load in loads:
        load.start()
    (
        tgt_pos,
        tgt_weight,
        tgt_pot,
        tgt_count,
        requests,
        src_pos,
        src_weight,
        src_pot,
        src_count,
        pair_count,
        src_row,
        slot_row,
    ) = held
    pairs = src_row.shape[1]

    for load in loads[:5]:
        load.wait()
    txs, tlevel, tlive = pack(tgt_pos, tgt_weight, tgt_pot, tgt_count)
    put_tiles(row_all.at[mx], txs + [tlevel])
    for r in range(n_clus):
        for m in range(REQ):
            own_req[r % nz, r // nz, m] = jnp.full((LANES,), requests[m, r], jnp.int32)

    pl.semaphore_wait(barrier, nx - 1 + nz - 1 + n_tgt - 1)

    q_copies = [
        send(own_req.at[at_z(d)], z_req.at[mz], q_send.at[d], q_recv.at[d], (mx, at_z(d), my, mc))
        for d in far_first(nz)
    ]
    x_copies = [
        send(row_all.at[mx], row_all.at[mx], x_send.at[d], x_recv.at[d], (at_x(d), mz, my, mc))
        for d in far_first(nx)
    ]
    for copy in x_copies + q_copies:
        copy.start()
    z_req[mz] = own_req[mz]
    for load in loads[5:]:
        load.wait()
    sxs, slevel, slive = pack(src_pos, src_weight, src_pot, src_count)
    put_tiles(src_all.at[mt], sxs + [slevel])
    s_copies = [
        send(src_all.at[mt], src_all.at[mt], s_send.at[d], s_recv.at[d], in_tgt(*d))
        for d in tgt_peers
    ]
    for copy in s_copies:
        copy.start()

    xs_near, zs_near = [0] + far_first(nx)[::-1], [0] + far_first(nz)[::-1]
    square = (pairs, pairs)
    down = rows_of(square)
    across = lax.broadcasted_iota(jnp.int32, square, 1)

    def column(v):
        v = jnp.where(down == across, jnp.broadcast_to(v, square), 0)
        return jnp.broadcast_to(jnp.sum(v, axis=1, keepdims=True), square)

    slot = slot_row[...]
    owner = slot >> 1
    behind_x = (mx - (owner >> (nz.bit_length() - 1))) & (nx - 1)
    behind_z = (mz - owner) & (nz - 1)
    place = slot & 1
    for i, d in enumerate(xs_near):
        place = place + jnp.where(behind_x == d, i * REQ, 0)
    for i, d in enumerate(zs_near):
        place = place + jnp.where(behind_z == d, i * nx * REQ, 0)
    dead = lax.broadcasted_iota(jnp.int32, (1, pairs), 1) >= pair_count[...]
    place = jnp.where(dead, 2 * pairs, place)
    theirs, mine = jnp.broadcast_to(place, square), column(place)
    before = (theirs < mine) | ((theirs == mine) & (across < down))
    rank = jnp.sum(jnp.where(before, 1, 0), axis=1, keepdims=True)
    hit = jnp.broadcast_to(rank, square) == across
    orders = []
    for i, (row, order, scalars) in enumerate(
        ((src_row, src_order, pair_src), (slot_row, slot_order, pair_slot))
    ):
        values = jnp.where(hit, column(row[...]), 0)
        order[...] = jnp.sum(values, axis=0, keepdims=True)
        orders.append(pltpu.make_async_copy(order, scalars, order_sem.at[i]))
        orders[-1].start()

    def choose(x, asked, put):
        blocks = [row_all[x, b * 8 : b * 8 + 8, :] for b in range(OWN)]
        for m in range(REQ):
            which = jnp.broadcast_to(z_req[asked, x, m : m + 1, :], (8, LANES))
            tile = blocks[0]
            for b in range(1, OWN):
                tile = jnp.where(which == b, blocks[b], tile)
            put[m] = tile

    for copy in q_copies:
        copy.wait_recv()
    z_copies = {}
    for dx in xs_near:
        x = lax.rem(mx + nx - dx, nx)
        if dx:
            x_copies[far_first(nx).index(dx)].wait_recv()
        for dz in far_first(nz):
            choose(x, at_z(dz), chosen.at[dz, dx])
            copy = send(
                chosen.at[dz, dx],
                tgt_all.at[mz, x],
                z_send.at[dz, dx],
                z_recv.at[dz, dx],
                (mx, at_z(dz), my, mc),
            )
            copy.start()
            z_copies[dz, dx] = copy
        choose(x, mz, tgt_all.at[mz, x])

    row8 = rows_of((8, BLK))
    ones3 = jnp.where(row8 < 3, 1.0, 0.0)
    zeros = jnp.zeros((8, BLK), f32)

    def prepare_tgt(z, dx):
        x = lax.rem(mx + nx - dx, nx)
        for m in range(REQ):
            v = unfold(tgt_all[z, x, m])
            hi, mid, lo = split3(jnp.where(row8 < 3, SCALE * v, jnp.where(row8 == 3, 1.0, 0.0)))
            lhi, lmid, llo = split3(jnp.broadcast_to(v[3:4, :], (8, BLK)))
            level = jnp.where(
                row8 == 0, lhi, jnp.where(row8 == 1, lmid, jnp.where(row8 == 2, llo, 0.0))
            )
            i = (x * nz + z) * REQ + m
            yy[i] = jnp.concatenate([hi, hi, mid, hi, lo, mid, level, zeros], axis=0).astype(bf16)
            tgt_w[i], tgt_w8[i] = sum_weights(v, row8)

    top = rows_of((8, LANES)) < 4

    def fold(s, rest):
        s = s[:8] + s[8:] + rest[:8] * (1.0 / LO)
        return jnp.where(top, s[:, :LANES], pltpu.roll(s[:, LANES:], 4, 0))

    def exponent(k):
        return lax.dot_general(
            yy[pair_slot[0, k]],
            xx[pair_src[0, k]],
            (((0,), (0,)), ((), ())),
            preferred_element_type=f32,
        )

    def pair(last, k, expo):
        later = exponent(jnp.minimum(k + 1, last))
        kern = jnp.exp2(expo)
        hi = kern.astype(bf16)
        lo = ((kern - hi.astype(f32)) * LO).astype(f8)
        j, i = pair_slot[0, k], pair_src[0, k]
        nt = (((1,), (1,)), ((), ()))
        s = fold(
            jnp.dot(tgt_w[j], hi, preferred_element_type=f32),
            jnp.dot(tgt_w8[j], lo, preferred_element_type=f32),
        )
        t = fold(
            lax.dot_general(src_w[i], hi, nt, preferred_element_type=f32),
            lax.dot_general(src_w8[i], lo, nt, preferred_element_type=f32),
        )
        src_parts[pl.ds(pl.multiple_of(k * 8, 8), 8), :] = s
        tgt_parts[pl.ds(pl.multiple_of(k * 8, 8), 8), :] = t
        return later

    def run(first, end):
        unroll = next(u for u in range(min(end - first, 56), 0, -1) if (end - first) % u == 0)
        lax.fori_loop(
            first, end, functools.partial(pair, end - 1), exponent(first), unroll=unroll
        )

    def arrive(dzs):
        for dz in dzs:
            for dx in xs_near:
                if dz:
                    z_copies[dz, dx].wait_recv()
                prepare_tgt(lax.rem(mz + nz - dz, nz), dx)

    arrive(zs_near[:1])
    for copy in s_copies:
        copy.wait_recv()

    def prepare_src(i, carry):
        v = unfold(src_all[i // OWN, pl.ds(pl.multiple_of(lax.rem(i, OWN) * 8, 8), 8), :])
        hi, mid, lo = split3(v)
        xx[i] = jnp.concatenate([hi, mid, hi, lo, hi, mid, ones3, zeros], axis=0).astype(bf16)
        src_w[i], src_w8[i] = sum_weights(v, row8)
        return carry

    lax.fori_loop(0, n_tgt * OWN, prepare_src, 0, unroll=2)

    for copy in orders:
        copy.wait()
    row_slots = nx * REQ
    run(0, row_slots)
    if nz > 2:
        arrive(zs_near[1:-1])
    arrive(zs_near[-1:])

    b_copies = [
        send(
            own_req.at[at_z(d[1]), at_x(d[0])],
            back_req.at[mr],
            b_send.at[d],
            b_recv.at[d],
            in_clus(*d),
        )
        for d in clus_peers
    ]
    for copy in b_copies:
        copy.start()

    run(row_slots, pairs)

    def combine(names, count, parts, put):
        at = lax.broadcasted_iota(jnp.int32, (count, pairs), 1)
        pick = (jnp.broadcast_to(names[...], (count, pairs)) == rows_of((count, pairs))) & (
            at < jnp.broadcast_to(pair_count[...], (count, pairs))
        )
        pick = jnp.where(pick, 1.0, 0.0).astype(bf16)
        for r in range(8):
            parts_r = parts[pl.ds(r, pairs, stride=8), :]
            hi = parts_r.astype(bf16)
            both = jnp.concatenate([hi, (parts_r - hi.astype(f32)).astype(bf16)], axis=1)
            s = jnp.dot(pick, both, preferred_element_type=f32)
            put[pl.ds(r, count, stride=8), :] = s[:, :LANES] + s[:, LANES:]

    combine(slot_order, slots, tgt_parts, tgt_send)

    def of_owner(ref, r):
        return ref.at[pl.ds(pl.multiple_of(r * (8 * REQ), 8 * REQ), 8 * REQ), :]

    t_copies = [
        send(
            of_owner(tgt_send, at_r(*d)),
            tgt_back.at[mr],
            t_send.at[d],
            t_recv.at[d],
            in_clus(*d),
        )
        for d in clus_peers
    ]
    for copy in t_copies:
        copy.start()

    combine(src_order, n_tgt * OWN, src_parts, src_send)

    def of_group(ref, t):
        return ref.at[pl.ds(pl.multiple_of(t * (8 * OWN), 8 * OWN), 8 * OWN), :]

    r_copies = [
        send(
            of_group(src_send, at_t(*d)),
            src_back.at[mt],
            r_send.at[d],
            r_recv.at[d],
            in_tgt(*d),
        )
        for d in tgt_peers
    ]
    for copy in r_copies:
        copy.start()
    def finish(xs, weight_ref, pot_ref, live, out):
        us = get_tiles(total)
        comps = [xs[c] * us[3] - us[c] for c in range(3)]
        comps.append(pot_ref[...] - ENTROPIC * us[3] / weight_ref[...])
        put_tiles(out, [jnp.where(live, comp, 0.0) for comp in comps])

    def add_tgt(sums, asked, tiles):
        for m in range(REQ):
            which = jnp.broadcast_to(asked[m : m + 1, :], (8, LANES))
            tile = tiles[m * 8 : m * 8 + 8, :]
            sums = [v + jnp.where(which == b, tile, 0.0) for b, v in enumerate(sums)]
        return sums

    sums = add_tgt(
        [jnp.zeros((8, LANES), f32)] * OWN, own_req.at[mz, mx], of_owner(tgt_send, mr)
    )
    for i in range(len(clus_peers) - 1, -1, -1):
        b_copies[i].wait_recv()
        t_copies[i].wait_recv()
        dx, dz = clus_peers[i]
        r = lax.rem(mx + nx - dx, nx) * nz + lax.rem(mz + nz - dz, nz)
        sums = add_tgt(sums, back_req.at[r], tgt_back.at[r])
    for b in range(OWN):
        total[b * 8 : b * 8 + 8, :] = sums[b]
    finish(txs, tgt_weight, tgt_pot, tlive, out_tgt)

    whole = of_group(src_send, mt)[...]
    for i in range(len(tgt_peers) - 1, -1, -1):
        r_copies[i].wait_recv()
        dy, dc = tgt_peers[i]
        whole = whole + src_back[lax.rem(my + ny - dy, ny) * nc + lax.rem(mc + nc - dc, nc)]
    total[...] = whole
    finish(sxs, src_weight, src_pot, slive, out_src)

    for copy in (
        x_copies + q_copies + s_copies + list(z_copies.values()) + b_copies + t_copies + r_copies
    ):
        copy.wait_send()


def write_out(src, tgt, src_pos, src_weight, tgt_pos, tgt_weight):
    for tiles, pos, weight in ((src, src_pos, src_weight), (tgt, tgt_pos, tgt_weight)):
        for q in range(2 * OWN):
            pos[:, q * LANES : q * LANES + LANES] = tiles[q * 4 : q * 4 + 3, :]
        weight[...] = tiles[pl.ds(3, 2 * OWN, stride=4), :]


def shards(
    dims,
    src_pos,
    src_weight,
    src_pot,
    src_count,
    tgt_pos,
    tgt_weight,
    tgt_pot,
    tgt_count,
    requests,
    pair_src,
    pair_slot,
    pair_count,
):
    nx, nz, ny, nc = dims
    n_tgt, n_clus = ny * nc, nx * nz
    slots = n_clus * REQ
    pairs = pair_src.shape[0]
    quarters = 2 * OWN

    def tall(v):
        return v.reshape(*v.shape[:-1], quarters, LANES)

    vmem = pl.BlockSpec(memory_space=pltpu.VMEM)
    dma = pltpu.SemaphoreType.DMA
    inputs = [
        tgt_pos,
        tall(tgt_weight),
        tall(tgt_pot),
        tgt_count,
        requests.T,
        src_pos,
        tall(src_weight),
        tall(src_pot),
        src_count,
        pair_count[None, :],
        pair_src[None, :],
        pair_slot[None, :],
    ]
    spaces = [pltpu.SMEM if i in (3, 4, 8) else pltpu.VMEM for i in range(12)]
    tiles = jax.ShapeDtypeStruct((8 * OWN, LANES), f32)
    sums = pl.pallas_call(
        functools.partial(kernel, dims),
        out_shape=[tiles, tiles],
        in_specs=[[pl.BlockSpec(memory_space=pltpu.HBM)] * len(inputs)],
        out_specs=[vmem] * 2,
        scratch_shapes=[
            [space(v.shape, v.dtype) for space, v in zip(spaces, inputs)],
            dma((len(inputs),)),
            pltpu.VMEM((1, pairs), jnp.int32),
            pltpu.VMEM((1, pairs), jnp.int32),
            pltpu.SMEM((1, pairs), jnp.int32),
            pltpu.SMEM((1, pairs), jnp.int32),
            dma((2,)),
            pltpu.VMEM((n_tgt, 8 * OWN, LANES), f32),
            pltpu.VMEM((nx, 8 * OWN, LANES), f32),
            pltpu.VMEM((nz, nx, REQ, 8, LANES), f32),
            pltpu.VMEM((nz, nx, REQ, 8, LANES), f32),
            pltpu.VMEM((nz, nx, REQ, LANES), jnp.int32),
            pltpu.VMEM((nz, nx, REQ, LANES), jnp.int32),
            pltpu.VMEM((n_clus, REQ, LANES), jnp.int32),
            pltpu.VMEM((n_tgt * OWN, 64, BLK), bf16),
            pltpu.VMEM((slots, 64, BLK), bf16),
            pltpu.VMEM((n_tgt * OWN, 16, BLK), bf16),
            pltpu.VMEM((slots, 16, BLK), bf16),
            pltpu.VMEM((n_tgt * OWN, 32, BLK), f8),
            pltpu.VMEM((slots, 32, BLK), f8),
            pltpu.VMEM((pairs * 8, LANES), f32),
            pltpu.VMEM((pairs * 8, LANES), f32),
            pltpu.VMEM((n_tgt * OWN * 8, LANES), f32),
            pltpu.VMEM((slots * 8, LANES), f32),
            pltpu.VMEM((n_tgt, 8 * OWN, LANES), f32),
            pltpu.VMEM((n_clus, 8 * REQ, LANES), f32),
            pltpu.VMEM((8 * OWN, LANES), f32),
            dma((nx,)),
            dma((nx,)),
            dma((nz,)),
            dma((nz,)),
            dma((ny, nc)),
            dma((ny, nc)),
            dma((nz, nx)),
            dma((nz, nx)),
            dma((nx, nz)),
            dma((nx, nz)),
            dma((nx, nz)),
            dma((nx, nz)),
            dma((ny, nc)),
            dma((ny, nc)),
        ],
        compiler_params=pltpu.CompilerParams(
            collective_id=0, has_side_effects=True, vmem_limit_bytes=48 << 20
        ),
    )(
        [
            v if v.size == 1 else pltpu.with_memory_space_constraint(v, pltpu.HBM)
            for v in inputs
        ]
    )
    pos = jax.ShapeDtypeStruct((3, quarters * LANES), f32)
    weight = jax.ShapeDtypeStruct((quarters, LANES), f32)
    outs = pl.pallas_call(
        write_out,
        out_shape=[pos, weight, pos, weight],
        in_specs=[vmem] * 2,
        compiler_params=pltpu.CompilerParams(vmem_limit_bytes=4 << 20),
    )(*sums)
    return outs[0], outs[1].reshape(-1), outs[2], outs[3].reshape(-1)


def solution(mesh):
    n_clus, n_tgt = mesh.shape["clus"], mesh.shape["tgt"]
    nx = math.isqrt(n_clus)
    dims = (nx, n_clus // nx, n_tgt // 2, 2)
    torus = Mesh(mesh.devices.reshape(dims), AXES)
    wide, flat = P(None, AXES), P(AXES)
    return jax.shard_map(
        functools.partial(shards, dims),
        mesh=torus,
        in_specs=(
            wide,
            flat,
            flat,
            flat,
            wide,
            flat,
            flat,
            flat,
            P(AXES, None),
            flat,
            flat,
            flat,
        ),
        out_specs=(wide, flat, wide, flat),
        check_vma=False,
    )
```

```python
import functools
import math

import jax
import jax.numpy as jnp
from jax import lax
from jax.experimental import pallas as pl
from jax.experimental.pallas import tpu as pltpu
from jax.sharding import Mesh
from jax.sharding import PartitionSpec as P

AXES = ("x", "z", "y", "core")
MESH = pl.DeviceIdType.MESH
BLK = 256
LANES = 128
OWN = 8
REQ = 2
ENTROPIC = 0.05
SCALE = 1.0 / (ENTROPIC * math.log(2.0))
DEAD = -1.0e4
VMEM = 67043328
f32 = jnp.float32
bf16 = jnp.bfloat16
f8 = jnp.float8_e4m3fn
LO = 2.0**13


def far_first(n):
    return sorted(range(1, n), key=lambda d: (-min(d, n - d), d))


def others(n, m):
    near = [(min(i, n - i) + min(j, m - j), i, j) for i in range(n) for j in range(m)]
    return [(i, j) for _, i, j in sorted(near, key=lambda v: (-v[0], v[1:])) if i or j]


def split3(v):
    hi = v.astype(bf16).astype(f32)
    rest = v - hi
    mid = rest.astype(bf16).astype(f32)
    return hi, mid, rest - mid


def rows_of(shape):
    return lax.broadcasted_iota(jnp.int32, shape, 0)


def pack(pos_ref, weight_ref, pot_ref, count_ref):
    quarters = weight_ref.shape[0]
    row = rows_of((quarters, LANES))
    lane = lax.broadcasted_iota(jnp.int32, (quarters, LANES), 1)
    counts = jnp.zeros((quarters, LANES), jnp.int32)
    for b in range(OWN):
        counts = jnp.where((row >> 1) == b, count_ref[b], counts)
    live = ((row & 1) * LANES + lane) < counts
    xs = [
        jnp.concatenate(
            [pos_ref[c : c + 1, q * LANES : q * LANES + LANES] for q in range(quarters)], axis=0
        )
        - 0.5
        for c in range(3)
    ]
    square = xs[0] * xs[0] + xs[1] * xs[1] + xs[2] * xs[2]
    level = SCALE * (pot_ref[...] - 0.5 * square) + jnp.log(weight_ref[...]) * (1.0 / math.log(2.0))
    return xs, jnp.where(live, level, DEAD), live


def put_tiles(tiles, comps):
    for c, comp in enumerate(comps):
        tiles[pl.ds(c, 2 * OWN, stride=4), :] = comp


def get_tiles(tiles):
    return [tiles[pl.ds(c, 2 * OWN, stride=4), :] for c in range(4)]


def unfold(tile):
    return jnp.concatenate([tile, pltpu.roll(tile, 4, 0)], axis=1)


def sum_weights(v, row):
    w = jnp.where((row & 3) == 3, 1.0, v)
    hi = w.astype(bf16).astype(f32)
    coarse = jnp.concatenate([w, jnp.zeros((24, BLK), f32)], axis=0).astype(f8)
    return jnp.concatenate([hi, w - hi], axis=0).astype(bf16), coarse


def kernel(
    dims,
    inputs,
    out_src,
    out_tgt,
    held,
    in_sem,
    src_order,
    slot_order,
    pair_src,
    pair_slot,
    order_sem,
    src_all,
    row_all,
    tgt_all,
    chosen,
    own_req,
    z_req,
    back_req,
    xx,
    yy,
    src_w,
    tgt_w,
    src_w8,
    tgt_w8,
    src_parts,
    tgt_parts,
    src_send,
    tgt_send,
    src_back,
    tgt_back,
    total,
    x_send,
    x_recv,
    q_send,
    q_recv,
    s_send,
    s_recv,
    z_send,
    z_recv,
    b_send,
    b_recv,
    t_send,
    t_recv,
    r_send,
    r_recv,
):
    nx, nz, ny, nc = dims
    n_tgt, n_clus = ny * nc, nx * nz
    slots = n_clus * REQ
    mx, mz, my, mc = (lax.axis_index(a) for a in AXES)
    mt, mr = my * nc + mc, mx * nz + mz

    def at_x(d):
        return lax.rem(mx + d, nx)

    def at_z(d):
        return lax.rem(mz + d, nz)

    def at_t(dy, dc):
        return lax.rem(my + dy, ny) * nc + lax.rem(mc + dc, nc)

    def at_r(dx, dz):
        return at_x(dx) * nz + at_z(dz)

    def in_tgt(dy, dc):
        return (mx, mz, lax.rem(my + dy, ny), lax.rem(mc + dc, nc))

    def in_clus(dx, dz):
        return (at_x(dx), at_z(dz), my, mc)

    tgt_peers = others(ny, nc)
    clus_peers = others(nx, nz)

    def send(src, dst, send_sem, recv_sem, device):
        return pltpu.make_async_remote_copy(
            src_ref=src,
            dst_ref=dst,
            send_sem=send_sem,
            recv_sem=recv_sem,
            device_id=device,
            device_id_type=MESH,
        )

    barrier = pltpu.get_barrier_semaphore()
    for d in range(1, nx):
        pl.semaphore_signal(barrier, inc=1, device_id=(at_x(d), mz, my, mc), device_id_type=MESH)
    for d in range(1, nz):
        pl.semaphore_signal(barrier, inc=1, device_id=(mx, at_z(d), my, mc), device_id_type=MESH)
    for d in tgt_peers:
        pl.semaphore_signal(barrier, inc=1, device_id=in_tgt(*d), device_id_type=MESH)

    loads = [
        pltpu.make_async_copy(src, dst, in_sem.at[i])
        for i, (src, dst) in enumerate(zip(inputs, held))
    ]
    for load in loads:
        load.start()
    (
        tgt_pos,
        tgt_weight,
        tgt_pot,
        tgt_count,
        requests,
        src_pos,
        src_weight,
        src_pot,
        src_count,
        pair_count,
        src_row,
        slot_row,
    ) = held
    pairs = src_row.shape[1]

    for load in loads[:5]:
        load.wait()
    txs, tlevel, tlive = pack(tgt_pos, tgt_weight, tgt_pot, tgt_count)
    put_tiles(row_all.at[mx], txs + [tlevel])
    for r in range(n_clus):
        for m in range(REQ):
            own_req[r % nz, r // nz, m] = jnp.full((LANES,), requests[m, r], jnp.int32)

    pl.semaphore_wait(barrier, nx - 1 + nz - 1 + n_tgt - 1)

    q_copies = [
        send(own_req.at[at_z(d)], z_req.at[mz], q_send.at[d], q_recv.at[d], (mx, at_z(d), my, mc))
        for d in far_first(nz)
    ]
    x_copies = [
        send(row_all.at[mx], row_all.at[mx], x_send.at[d], x_recv.at[d], (at_x(d), mz, my, mc))
        for d in far_first(nx)
    ]
    for copy in x_copies + q_copies:
        copy.start()
    z_req[mz] = own_req[mz]
    for load in loads[5:]:
        load.wait()
    sxs, slevel, slive = pack(src_pos, src_weight, src_pot, src_count)
    put_tiles(src_all.at[mt], sxs + [slevel])
    s_copies = [
        send(src_all.at[mt], src_all.at[mt], s_send.at[d], s_recv.at[d], in_tgt(*d))
        for d in tgt_peers
    ]
    for copy in s_copies:
        copy.start()

    xs_near, zs_near = [0] + far_first(nx)[::-1], [0] + far_first(nz)[::-1]
    square = (pairs, pairs)
    down = rows_of(square)
    across = lax.broadcasted_iota(jnp.int32, square, 1)

    def column(v):
        v = jnp.where(down == across, jnp.broadcast_to(v, square), 0)
        return jnp.broadcast_to(jnp.sum(v, axis=1, keepdims=True), square)

    slot = slot_row[...]
    owner = slot >> 1
    behind_x = (mx - (owner >> (nz.bit_length() - 1))) & (nx - 1)
    behind_z = (mz - owner) & (nz - 1)
    place = slot & 1
    for i, d in enumerate(xs_near):
        place = place + jnp.where(behind_x == d, i * REQ, 0)
    for i, d in enumerate(zs_near):
        place = place + jnp.where(behind_z == d, i * nx * REQ, 0)
    dead = lax.broadcasted_iota(jnp.int32, (1, pairs), 1) >= pair_count[...]
    place = jnp.where(dead, 2 * pairs, place)
    theirs, mine = jnp.broadcast_to(place, square), column(place)
    before = (theirs < mine) | ((theirs == mine) & (across < down))
    rank = jnp.sum(jnp.where(before, 1, 0), axis=1, keepdims=True)
    hit = jnp.broadcast_to(rank, square) == across
    orders = []
    for i, (row, order, scalars) in enumerate(
        ((src_row, src_order, pair_src), (slot_row, slot_order, pair_slot))
    ):
        values = jnp.where(hit, column(row[...]), 0)
        order[...] = jnp.sum(values, axis=0, keepdims=True)
        orders.append(pltpu.make_async_copy(order, scalars, order_sem.at[i]))
        orders[-1].start()

    def choose(x, asked, put):
        blocks = [row_all[x, b * 8 : b * 8 + 8, :] for b in range(OWN)]
        for m in range(REQ):
            which = jnp.broadcast_to(z_req[asked, x, m : m + 1, :], (8, LANES))
            tile = blocks[0]
            for b in range(1, OWN):
                tile = jnp.where(which == b, blocks[b], tile)
            put[m] = tile

    for copy in q_copies:
        copy.wait_recv()
    z_copies = {}
    for dx in xs_near:
        x = lax.rem(mx + nx - dx, nx)
        if dx:
            x_copies[far_first(nx).index(dx)].wait_recv()
        for dz in far_first(nz):
            choose(x, at_z(dz), chosen.at[dz, dx])
            copy = send(
                chosen.at[dz, dx],
                tgt_all.at[mz, x],
                z_send.at[dz, dx],
                z_recv.at[dz, dx],
                (mx, at_z(dz), my, mc),
            )
            copy.start()
            z_copies[dz, dx] = copy
        choose(x, mz, tgt_all.at[mz, x])

    row8 = rows_of((8, BLK))

    def prepare_tgt(z, dx):
        x = lax.rem(mx + nx - dx, nx)
        for m in range(REQ):
            v = unfold(tgt_all[z, x, m])
            level = jnp.where(row8 == 4, pltpu.roll(v, 1, 0), jnp.where(row8 == 3, 1.0, 0.0))
            hi, mid, lo = split3(jnp.where(row8 < 3, SCALE * v, level))
            i = (x * nz + z) * REQ + m
            yy[i] = jnp.concatenate([hi, hi, mid, hi, lo, mid], axis=0).astype(bf16)
            tgt_w[i], tgt_w8[i] = sum_weights(v, row8)

    top = rows_of((8, LANES)) < 4

    def fold(s, rest):
        s = s[:8] + s[8:] + rest[:8] * (1.0 / LO)
        return jnp.where(top, s[:, :LANES], pltpu.roll(s[:, LANES:], 4, 0))

    def exponent(k):
        return lax.dot_general(
            yy[pair_slot[0, k]],
            xx[pair_src[0, k]],
            (((0,), (0,)), ((), ())),
            preferred_element_type=f32,
        )

    def pair(last, k, expo):
        later = exponent(jnp.minimum(k + 1, last))
        kern = jnp.exp2(expo)
        hi = kern.astype(bf16)
        lo = ((kern - hi.astype(f32)) * LO).astype(f8)
        j, i = pair_slot[0, k], pair_src[0, k]
        nt = (((1,), (1,)), ((), ()))
        s = fold(
            jnp.dot(tgt_w[j], hi, preferred_element_type=f32),
            jnp.dot(tgt_w8[j], lo, preferred_element_type=f32),
        )
        t = fold(
            lax.dot_general(src_w[i], hi, nt, preferred_element_type=f32),
            lax.dot_general(src_w8[i], lo, nt, preferred_element_type=f32),
        )
        src_parts[pl.ds(pl.multiple_of(k * 8, 8), 8), :] = s
        tgt_parts[pl.ds(pl.multiple_of(k * 8, 8), 8), :] = t
        return later

    def run(first, end):
        unroll = next(u for u in range(min(end - first, 56), 0, -1) if (end - first) % u == 0)
        lax.fori_loop(
            first, end, functools.partial(pair, end - 1), exponent(first), unroll=unroll
        )

    def arrive(dzs):
        for dz in dzs:
            for dx in xs_near:
                if dz:
                    z_copies[dz, dx].wait_recv()
                prepare_tgt(lax.rem(mz + nz - dz, nz), dx)

    arrive(zs_near[:1])
    for copy in s_copies:
        copy.wait_recv()

    def prepare_src(i, carry):
        v = unfold(src_all[i // OWN, pl.ds(pl.multiple_of(lax.rem(i, OWN) * 8, 8), 8), :])
        hi, mid, lo = split3(jnp.where(row8 == 4, 1.0, v))
        xx[i] = jnp.concatenate([hi, mid, hi, lo, hi, mid], axis=0).astype(bf16)
        src_w[i], src_w8[i] = sum_weights(v, row8)
        return carry

    lax.fori_loop(0, n_tgt * OWN, prepare_src, 0, unroll=2)

    for copy in orders:
        copy.wait()
    row_slots = nx * REQ
    run(0, row_slots)
    if nz > 2:
        arrive(zs_near[1:-1])
    arrive(zs_near[-1:])

    b_copies = [
        send(
            own_req.at[at_z(d[1]), at_x(d[0])],
            back_req.at[mr],
            b_send.at[d],
            b_recv.at[d],
            in_clus(*d),
        )
        for d in clus_peers
    ]
    for copy in b_copies:
        copy.start()

    run(row_slots, pairs)

    def combine(names, count, parts, put):
        at = lax.broadcasted_iota(jnp.int32, (count, pairs), 1)
        pick = (jnp.broadcast_to(names[...], (count, pairs)) == rows_of((count, pairs))) & (
            at < jnp.broadcast_to(pair_count[...], (count, pairs))
        )
        pick = jnp.where(pick, 1.0, 0.0).astype(bf16)
        for r in range(8):
            parts_r = parts[pl.ds(r, pairs, stride=8), :]
            hi = parts_r.astype(bf16)
            both = jnp.concatenate([hi, (parts_r - hi.astype(f32)).astype(bf16)], axis=1)
            s = jnp.dot(pick, both, preferred_element_type=f32)
            put[pl.ds(r, count, stride=8), :] = s[:, :LANES] + s[:, LANES:]

    combine(slot_order, slots, tgt_parts, tgt_send)

    def of_owner(ref, r):
        return ref.at[pl.ds(pl.multiple_of(r * (8 * REQ), 8 * REQ), 8 * REQ), :]

    t_copies = [
        send(
            of_owner(tgt_send, at_r(*d)),
            tgt_back.at[mr],
            t_send.at[d],
            t_recv.at[d],
            in_clus(*d),
        )
        for d in clus_peers
    ]
    for copy in t_copies:
        copy.start()

    combine(src_order, n_tgt * OWN, src_parts, src_send)

    def of_group(ref, t):
        return ref.at[pl.ds(pl.multiple_of(t * (8 * OWN), 8 * OWN), 8 * OWN), :]

    r_copies = [
        send(
            of_group(src_send, at_t(*d)),
            src_back.at[mt],
            r_send.at[d],
            r_recv.at[d],
            in_tgt(*d),
        )
        for d in tgt_peers
    ]
    for copy in r_copies:
        copy.start()
    def finish(xs, weight_ref, pot_ref, live, out):
        us = get_tiles(total)
        comps = [xs[c] * us[3] - us[c] for c in range(3)]
        comps.append(pot_ref[...] - ENTROPIC * us[3] / weight_ref[...])
        put_tiles(out, [jnp.where(live, comp, 0.0) for comp in comps])

    def add_tgt(sums, asked, tiles):
        for m in range(REQ):
            which = jnp.broadcast_to(asked[m : m + 1, :], (8, LANES))
            tile = tiles[m * 8 : m * 8 + 8, :]
            sums = [v + jnp.where(which == b, tile, 0.0) for b, v in enumerate(sums)]
        return sums

    sums = add_tgt(
        [jnp.zeros((8, LANES), f32)] * OWN, own_req.at[mz, mx], of_owner(tgt_send, mr)
    )
    for i in range(len(clus_peers) - 1, -1, -1):
        b_copies[i].wait_recv()
        t_copies[i].wait_recv()
        dx, dz = clus_peers[i]
        r = lax.rem(mx + nx - dx, nx) * nz + lax.rem(mz + nz - dz, nz)
        sums = add_tgt(sums, back_req.at[r], tgt_back.at[r])
    for b in range(OWN):
        total[b * 8 : b * 8 + 8, :] = sums[b]
    finish(txs, tgt_weight, tgt_pot, tlive, out_tgt)

    whole = of_group(src_send, mt)[...]
    for i in range(len(tgt_peers) - 1, -1, -1):
        r_copies[i].wait_recv()
        dy, dc = tgt_peers[i]
        whole = whole + src_back[lax.rem(my + ny - dy, ny) * nc + lax.rem(mc + nc - dc, nc)]
    total[...] = whole
    finish(sxs, src_weight, src_pot, slive, out_src)

    for copy in (
        x_copies + q_copies + s_copies + list(z_copies.values()) + b_copies + t_copies + r_copies
    ):
        copy.wait_send()


def write_out(src, tgt, src_pos, src_weight, tgt_pos, tgt_weight):
    for tiles, pos, weight in ((src, src_pos, src_weight), (tgt, tgt_pos, tgt_weight)):
        for q in range(2 * OWN):
            pos[:, q * LANES : q * LANES + LANES] = tiles[q * 4 : q * 4 + 3, :]
        weight[...] = tiles[pl.ds(3, 2 * OWN, stride=4), :]


def shards(
    dims,
    src_pos,
    src_weight,
    src_pot,
    src_count,
    tgt_pos,
    tgt_weight,
    tgt_pot,
    tgt_count,
    requests,
    pair_src,
    pair_slot,
    pair_count,
):
    nx, nz, ny, nc = dims
    n_tgt, n_clus = ny * nc, nx * nz
    slots = n_clus * REQ
    pairs = pair_src.shape[0]
    quarters = 2 * OWN

    def tall(v):
        return v.reshape(*v.shape[:-1], quarters, LANES)

    vmem = pl.BlockSpec(memory_space=pltpu.VMEM)
    dma = pltpu.SemaphoreType.DMA
    inputs = [
        tgt_pos,
        tall(tgt_weight),
        tall(tgt_pot),
        tgt_count,
        requests.T,
        src_pos,
        tall(src_weight),
        tall(src_pot),
        src_count,
        pair_count[None, :],
        pair_src[None, :],
        pair_slot[None, :],
    ]
    spaces = [pltpu.SMEM if i in (3, 4, 8) else pltpu.VMEM for i in range(12)]
    tiles = jax.ShapeDtypeStruct((8 * OWN, LANES), f32)
    sums = pl.pallas_call(
        functools.partial(kernel, dims),
        out_shape=[tiles, tiles],
        in_specs=[[pl.BlockSpec(memory_space=pltpu.HBM)] * len(inputs)],
        out_specs=[vmem] * 2,
        scratch_shapes=[
            [space(v.shape, v.dtype) for space, v in zip(spaces, inputs)],
            dma((len(inputs),)),
            pltpu.VMEM((1, pairs), jnp.int32),
            pltpu.VMEM((1, pairs), jnp.int32),
            pltpu.SMEM((1, pairs), jnp.int32),
            pltpu.SMEM((1, pairs), jnp.int32),
            dma((2,)),
            pltpu.VMEM((n_tgt, 8 * OWN, LANES), f32),
            pltpu.VMEM((nx, 8 * OWN, LANES), f32),
            pltpu.VMEM((nz, nx, REQ, 8, LANES), f32),
            pltpu.VMEM((nz, nx, REQ, 8, LANES), f32),
            pltpu.VMEM((nz, nx, REQ, LANES), jnp.int32),
            pltpu.VMEM((nz, nx, REQ, LANES), jnp.int32),
            pltpu.VMEM((n_clus, REQ, LANES), jnp.int32),
            pltpu.VMEM((n_tgt * OWN, 48, BLK), bf16),
            pltpu.VMEM((slots, 48, BLK), bf16),
            pltpu.VMEM((n_tgt * OWN, 16, BLK), bf16),
            pltpu.VMEM((slots, 16, BLK), bf16),
            pltpu.VMEM((n_tgt * OWN, 32, BLK), f8),
            pltpu.VMEM((slots, 32, BLK), f8),
            pltpu.VMEM((pairs * 8, LANES), f32),
            pltpu.VMEM((pairs * 8, LANES), f32),
            pltpu.VMEM((n_tgt * OWN * 8, LANES), f32),
            pltpu.VMEM((slots * 8, LANES), f32),
            pltpu.VMEM((n_tgt, 8 * OWN, LANES), f32),
            pltpu.VMEM((n_clus, 8 * REQ, LANES), f32),
            pltpu.VMEM((8 * OWN, LANES), f32),
            dma((nx,)),
            dma((nx,)),
            dma((nz,)),
            dma((nz,)),
            dma((ny, nc)),
            dma((ny, nc)),
            dma((nz, nx)),
            dma((nz, nx)),
            dma((nx, nz)),
            dma((nx, nz)),
            dma((nx, nz)),
            dma((nx, nz)),
            dma((ny, nc)),
            dma((ny, nc)),
        ],
        compiler_params=pltpu.CompilerParams(
            collective_id=0, has_side_effects=True, vmem_limit_bytes=48 << 20
        ),
    )(
        [
            v if v.size == 1 else pltpu.with_memory_space_constraint(v, pltpu.HBM)
            for v in inputs
        ]
    )
    pos = jax.ShapeDtypeStruct((3, quarters * LANES), f32)
    weight = jax.ShapeDtypeStruct((quarters, LANES), f32)
    outs = pl.pallas_call(
        write_out,
        out_shape=[pos, weight, pos, weight],
        in_specs=[vmem] * 2,
        compiler_params=pltpu.CompilerParams(vmem_limit_bytes=4 << 20),
    )(*sums)
    return outs[0], outs[1].reshape(-1), outs[2], outs[3].reshape(-1)


def solution(mesh):
    n_clus, n_tgt = mesh.shape["clus"], mesh.shape["tgt"]
    nx = math.isqrt(n_clus)
    dims = (nx, n_clus // nx, n_tgt // 2, 2)
    torus = Mesh(mesh.devices.reshape(dims), AXES)
    wide, flat = P(None, AXES), P(AXES)
    return jax.shard_map(
        functools.partial(shards, dims),
        mesh=torus,
        in_specs=(
            wide,
            flat,
            flat,
            flat,
            wide,
            flat,
            flat,
            flat,
            P(AXES, None),
            flat,
            flat,
            flat,
        ),
        out_specs=(wide, flat, wide, flat),
        check_vma=False,
    )
```

```python
import functools
import math

import jax
import jax.numpy as jnp
from jax import lax
from jax.experimental import pallas as pl
from jax.experimental.pallas import tpu as pltpu
from jax.sharding import Mesh
from jax.sharding import PartitionSpec as P

AXES = ("x", "z", "y", "core")
MESH = pl.DeviceIdType.MESH
BLK = 256
LANES = 128
OWN = 8
REQ = 2
ENTROPIC = 0.05
SCALE = 1.0 / (ENTROPIC * math.log(2.0))
DEAD = -1.0e4
VMEM = 67043328
f32 = jnp.float32
bf16 = jnp.bfloat16
f8 = jnp.float8_e4m3fn
LO = 2.0**13


def far_first(n):
    return sorted(range(1, n), key=lambda d: (-min(d, n - d), d))


def others(n, m):
    near = [(min(i, n - i) + min(j, m - j), i, j) for i in range(n) for j in range(m)]
    return [(i, j) for _, i, j in sorted(near, key=lambda v: (-v[0], v[1:])) if i or j]


def split3(v):
    hi = v.astype(bf16).astype(f32)
    rest = v - hi
    mid = rest.astype(bf16).astype(f32)
    return hi, mid, rest - mid


def rows_of(shape):
    return lax.broadcasted_iota(jnp.int32, shape, 0)


def pack(pos_ref, weight_ref, pot_ref, count_ref):
    quarters = weight_ref.shape[0]
    row = rows_of((quarters, LANES))
    lane = lax.broadcasted_iota(jnp.int32, (quarters, LANES), 1)
    counts = jnp.zeros((quarters, LANES), jnp.int32)
    for b in range(OWN):
        counts = jnp.where((row >> 1) == b, count_ref[b], counts)
    live = ((row & 1) * LANES + lane) < counts
    xs = [
        jnp.concatenate(
            [pos_ref[c : c + 1, q * LANES : q * LANES + LANES] for q in range(quarters)], axis=0
        )
        - 0.5
        for c in range(3)
    ]
    square = xs[0] * xs[0] + xs[1] * xs[1] + xs[2] * xs[2]
    level = SCALE * (pot_ref[...] - 0.5 * square) + jnp.log(weight_ref[...]) * (1.0 / math.log(2.0))
    return xs, jnp.where(live, level, DEAD), live


def put_tiles(tiles, comps):
    for c, comp in enumerate(comps):
        tiles[pl.ds(c, 2 * OWN, stride=4), :] = comp


def get_tiles(tiles):
    return [tiles[pl.ds(c, 2 * OWN, stride=4), :] for c in range(4)]


def unfold(tile):
    return jnp.concatenate([tile, pltpu.roll(tile, 4, 0)], axis=1)


def sum_weights(v, row):
    w = jnp.where((row & 3) == 3, 1.0, v)
    hi = w.astype(bf16).astype(f32)
    coarse = jnp.concatenate([w, jnp.zeros((24, BLK), f32)], axis=0).astype(f8)
    return jnp.concatenate([hi, w - hi], axis=0).astype(bf16), coarse


def kernel(
    dims,
    inputs,
    out_src,
    out_tgt,
    held,
    in_sem,
    src_order,
    slot_order,
    pair_src,
    pair_slot,
    order_sem,
    src_all,
    row_all,
    tgt_all,
    chosen,
    own_req,
    z_req,
    back_req,
    xx,
    yy,
    src_w,
    tgt_w,
    src_w8,
    tgt_w8,
    src_parts,
    tgt_parts,
    src_send,
    tgt_send,
    src_back,
    tgt_back,
    total,
    x_send,
    x_recv,
    q_send,
    q_recv,
    s_send,
    s_recv,
    z_send,
    z_recv,
    b_send,
    b_recv,
    t_send,
    t_recv,
    r_send,
    r_recv,
):
    nx, nz, ny, nc = dims
    n_tgt, n_clus = ny * nc, nx * nz
    slots = n_clus * REQ
    mx, mz, my, mc = (lax.axis_index(a) for a in AXES)
    mt, mr = my * nc + mc, mx * nz + mz

    def at_x(d):
        return lax.rem(mx + d, nx)

    def at_z(d):
        return lax.rem(mz + d, nz)

    def at_t(dy, dc):
        return lax.rem(my + dy, ny) * nc + lax.rem(mc + dc, nc)

    def at_r(dx, dz):
        return at_x(dx) * nz + at_z(dz)

    def in_tgt(dy, dc):
        return (mx, mz, lax.rem(my + dy, ny), lax.rem(mc + dc, nc))

    def in_clus(dx, dz):
        return (at_x(dx), at_z(dz), my, mc)

    tgt_peers = others(ny, nc)
    clus_peers = others(nx, nz)

    def send(src, dst, send_sem, recv_sem, device):
        return pltpu.make_async_remote_copy(
            src_ref=src,
            dst_ref=dst,
            send_sem=send_sem,
            recv_sem=recv_sem,
            device_id=device,
            device_id_type=MESH,
        )

    barrier = pltpu.get_barrier_semaphore()
    for d in range(1, nx):
        pl.semaphore_signal(barrier, inc=1, device_id=(at_x(d), mz, my, mc), device_id_type=MESH)
    for d in range(1, nz):
        pl.semaphore_signal(barrier, inc=1, device_id=(mx, at_z(d), my, mc), device_id_type=MESH)
    for d in tgt_peers:
        pl.semaphore_signal(barrier, inc=1, device_id=in_tgt(*d), device_id_type=MESH)

    loads = [
        pltpu.make_async_copy(src, dst, in_sem.at[i])
        for i, (src, dst) in enumerate(zip(inputs, held))
    ]
    for load in loads:
        load.start()
    (
        tgt_pos,
        tgt_weight,
        tgt_pot,
        tgt_count,
        requests,
        src_pos,
        src_weight,
        src_pot,
        src_count,
        pair_count,
        src_row,
        slot_row,
    ) = held
    pairs = src_row.shape[1]

    for load in loads[:5]:
        load.wait()
    txs, tlevel, tlive = pack(tgt_pos, tgt_weight, tgt_pot, tgt_count)
    put_tiles(row_all.at[mx], txs + [tlevel])
    for r in range(n_clus):
        for m in range(REQ):
            own_req[r % nz, r // nz, m] = jnp.full((LANES,), requests[m, r], jnp.int32)

    pl.semaphore_wait(barrier, nx - 1 + nz - 1 + n_tgt - 1)

    q_copies = [
        send(own_req.at[at_z(d)], z_req.at[mz], q_send.at[d], q_recv.at[d], (mx, at_z(d), my, mc))
        for d in far_first(nz)
    ]
    x_copies = [
        send(row_all.at[mx], row_all.at[mx], x_send.at[d], x_recv.at[d], (at_x(d), mz, my, mc))
        for d in far_first(nx)
    ]
    for copy in x_copies + q_copies:
        copy.start()
    z_req[mz] = own_req[mz]
    for load in loads[5:]:
        load.wait()
    sxs, slevel, slive = pack(src_pos, src_weight, src_pot, src_count)
    put_tiles(src_all.at[mt], sxs + [slevel])
    s_copies = [
        send(src_all.at[mt], src_all.at[mt], s_send.at[d], s_recv.at[d], in_tgt(*d))
        for d in tgt_peers
    ]
    for copy in s_copies:
        copy.start()

    xs_near, zs_near = [0] + far_first(nx)[::-1], [0] + far_first(nz)[::-1]
    square = (pairs, pairs)
    down = rows_of(square)
    across = lax.broadcasted_iota(jnp.int32, square, 1)

    def column(v):
        v = jnp.where(down == across, jnp.broadcast_to(v, square), 0)
        return jnp.broadcast_to(jnp.sum(v, axis=1, keepdims=True), square)

    slot = slot_row[...]
    owner = slot >> 1
    behind_x = (mx - (owner >> (nz.bit_length() - 1))) & (nx - 1)
    behind_z = (mz - owner) & (nz - 1)
    place = slot & 1
    for i, d in enumerate(xs_near):
        place = place + jnp.where(behind_x == d, i * REQ, 0)
    for i, d in enumerate(zs_near):
        place = place + jnp.where(behind_z == d, i * nx * REQ, 0)
    dead = lax.broadcasted_iota(jnp.int32, (1, pairs), 1) >= pair_count[...]
    place = jnp.where(dead, 2 * pairs, place)
    theirs, mine = jnp.broadcast_to(place, square), column(place)
    before = (theirs < mine) | ((theirs == mine) & (across < down))
    rank = jnp.sum(jnp.where(before, 1, 0), axis=1, keepdims=True)
    hit = jnp.broadcast_to(rank, square) == across
    orders = []
    for i, (row, order, scalars) in enumerate(
        ((src_row, src_order, pair_src), (slot_row, slot_order, pair_slot))
    ):
        values = jnp.where(hit, column(row[...]), 0)
        order[...] = jnp.sum(values, axis=0, keepdims=True)
        orders.append(pltpu.make_async_copy(order, scalars, order_sem.at[i]))
        orders[-1].start()

    def choose(x, asked, put):
        blocks = [row_all[x, b * 8 : b * 8 + 8, :] for b in range(OWN)]
        for m in range(REQ):
            which = jnp.broadcast_to(z_req[asked, x, m : m + 1, :], (8, LANES))
            tile = blocks[0]
            for b in range(1, OWN):
                tile = jnp.where(which == b, blocks[b], tile)
            put[m] = tile

    for copy in q_copies:
        copy.wait_recv()
    z_copies = {}
    for dx in xs_near:
        x = lax.rem(mx + nx - dx, nx)
        if dx:
            x_copies[far_first(nx).index(dx)].wait_recv()
        for dz in far_first(nz):
            choose(x, at_z(dz), chosen.at[dz, dx])
            copy = send(
                chosen.at[dz, dx],
                tgt_all.at[mz, x],
                z_send.at[dz, dx],
                z_recv.at[dz, dx],
                (mx, at_z(dz), my, mc),
            )
            copy.start()
            z_copies[dz, dx] = copy
        choose(x, mz, tgt_all.at[mz, x])

    row8 = rows_of((8, BLK))

    def prepare_tgt(z, dx):
        x = lax.rem(mx + nx - dx, nx)
        for m in range(REQ):
            v = unfold(tgt_all[z, x, m])
            level = jnp.where(row8 == 4, pltpu.roll(v, 1, 0), jnp.where(row8 == 3, 1.0, 0.0))
            hi, mid, lo = split3(jnp.where(row8 < 3, SCALE * v, level))
            i = (x * nz + z) * REQ + m
            yy[i] = jnp.concatenate([hi, hi, mid, hi, lo, mid], axis=0).astype(bf16)
            tgt_w[i], tgt_w8[i] = sum_weights(v, row8)

    top = rows_of((8, LANES)) < 4

    def fold(s, rest):
        s = s[:8] + s[8:] + rest[:8] * (1.0 / LO)
        return jnp.where(top, s[:, :LANES], pltpu.roll(s[:, LANES:], 4, 0))

    def exponent(k):
        return lax.dot_general(
            yy[pair_slot[0, k]],
            xx[pair_src[0, k]],
            (((0,), (0,)), ((), ())),
            preferred_element_type=f32,
        )

    def pair(last, k, expo):
        later = exponent(jnp.minimum(k + 1, last))
        kern = jnp.exp2(expo)
        hi = kern.astype(bf16)
        lo = ((kern - hi.astype(f32)) * LO).astype(f8)
        j, i = pair_slot[0, k], pair_src[0, k]
        nt = (((1,), (1,)), ((), ()))
        s = fold(
            jnp.dot(tgt_w[j], hi, preferred_element_type=f32),
            jnp.dot(tgt_w8[j], lo, preferred_element_type=f32),
        )
        t = fold(
            lax.dot_general(src_w[i], hi, nt, preferred_element_type=f32),
            lax.dot_general(src_w8[i], lo, nt, preferred_element_type=f32),
        )
        src_parts[pl.ds(pl.multiple_of(k * 8, 8), 8), :] = s
        tgt_parts[pl.ds(pl.multiple_of(k * 8, 8), 8), :] = t
        return later

    def run(first, end):
        unroll = next(u for u in range(min(end - first, 56), 0, -1) if (end - first) % u == 0)
        lax.fori_loop(
            first, end, functools.partial(pair, end - 1), exponent(first), unroll=unroll
        )

    def arrive(dzs):
        for dz in dzs:
            for dx in xs_near:
                if dz:
                    z_copies[dz, dx].wait_recv()
                prepare_tgt(lax.rem(mz + nz - dz, nz), dx)

    arrive(zs_near[:1])
    def prepare_src(t, b, carry):
        i = t * OWN + b
        v = unfold(src_all[t, pl.ds(pl.multiple_of(b * 8, 8), 8), :])
        hi, mid, lo = split3(jnp.where(row8 == 4, 1.0, v))
        xx[i] = jnp.concatenate([hi, mid, hi, lo, hi, mid], axis=0).astype(bf16)
        src_w[i], src_w8[i] = sum_weights(v, row8)
        return carry

    lax.fori_loop(0, OWN, functools.partial(prepare_src, mt), 0, unroll=2)
    for copy, (dy, dc) in zip(s_copies[::-1], tgt_peers[::-1]):
        copy.wait_recv()
        t = lax.rem(my + ny - dy, ny) * nc + lax.rem(mc + nc - dc, nc)
        lax.fori_loop(0, OWN, functools.partial(prepare_src, t), 0, unroll=2)

    for copy in orders:
        copy.wait()
    row_slots = nx * REQ
    run(0, row_slots)
    if nz > 2:
        arrive(zs_near[1:-1])
    arrive(zs_near[-1:])

    b_copies = [
        send(
            own_req.at[at_z(d[1]), at_x(d[0])],
            back_req.at[mr],
            b_send.at[d],
            b_recv.at[d],
            in_clus(*d),
        )
        for d in clus_peers
    ]
    for copy in b_copies:
        copy.start()

    run(row_slots, pairs)

    def combine(names, count, parts, put):
        at = lax.broadcasted_iota(jnp.int32, (count, pairs), 1)
        pick = (jnp.broadcast_to(names[...], (count, pairs)) == rows_of((count, pairs))) & (
            at < jnp.broadcast_to(pair_count[...], (count, pairs))
        )
        pick = jnp.where(pick, 1.0, 0.0).astype(bf16)
        for r in range(8):
            parts_r = parts[pl.ds(r, pairs, stride=8), :]
            hi = parts_r.astype(bf16)
            both = jnp.concatenate([hi, (parts_r - hi.astype(f32)).astype(bf16)], axis=1)
            s = jnp.dot(pick, both, preferred_element_type=f32)
            put[pl.ds(r, count, stride=8), :] = s[:, :LANES] + s[:, LANES:]

    combine(slot_order, slots, tgt_parts, tgt_send)

    def of_owner(ref, r):
        return ref.at[pl.ds(pl.multiple_of(r * (8 * REQ), 8 * REQ), 8 * REQ), :]

    t_copies = [
        send(
            of_owner(tgt_send, at_r(*d)),
            tgt_back.at[mr],
            t_send.at[d],
            t_recv.at[d],
            in_clus(*d),
        )
        for d in clus_peers
    ]
    for copy in t_copies:
        copy.start()

    combine(src_order, n_tgt * OWN, src_parts, src_send)

    def of_group(ref, t):
        return ref.at[pl.ds(pl.multiple_of(t * (8 * OWN), 8 * OWN), 8 * OWN), :]

    r_copies = [
        send(
            of_group(src_send, at_t(*d)),
            src_back.at[mt],
            r_send.at[d],
            r_recv.at[d],
            in_tgt(*d),
        )
        for d in tgt_peers
    ]
    for copy in r_copies:
        copy.start()
    def finish(xs, weight_ref, pot_ref, live, out):
        us = get_tiles(total)
        comps = [xs[c] * us[3] - us[c] for c in range(3)]
        comps.append(pot_ref[...] - ENTROPIC * us[3] / weight_ref[...])
        put_tiles(out, [jnp.where(live, comp, 0.0) for comp in comps])

    def add_tgt(sums, asked, tiles):
        for m in range(REQ):
            which = jnp.broadcast_to(asked[m : m + 1, :], (8, LANES))
            tile = tiles[m * 8 : m * 8 + 8, :]
            sums = [v + jnp.where(which == b, tile, 0.0) for b, v in enumerate(sums)]
        return sums

    sums = add_tgt(
        [jnp.zeros((8, LANES), f32)] * OWN, own_req.at[mz, mx], of_owner(tgt_send, mr)
    )
    for i in range(len(clus_peers) - 1, -1, -1):
        b_copies[i].wait_recv()
        t_copies[i].wait_recv()
        dx, dz = clus_peers[i]
        r = lax.rem(mx + nx - dx, nx) * nz + lax.rem(mz + nz - dz, nz)
        sums = add_tgt(sums, back_req.at[r], tgt_back.at[r])
    for b in range(OWN):
        total[b * 8 : b * 8 + 8, :] = sums[b]
    finish(txs, tgt_weight, tgt_pot, tlive, out_tgt)

    whole = of_group(src_send, mt)[...]
    for i in range(len(tgt_peers) - 1, -1, -1):
        r_copies[i].wait_recv()
        dy, dc = tgt_peers[i]
        whole = whole + src_back[lax.rem(my + ny - dy, ny) * nc + lax.rem(mc + nc - dc, nc)]
    total[...] = whole
    finish(sxs, src_weight, src_pot, slive, out_src)

    for copy in (
        x_copies + q_copies + s_copies + list(z_copies.values()) + b_copies + t_copies + r_copies
    ):
        copy.wait_send()


def write_out(src, tgt, src_pos, src_weight, tgt_pos, tgt_weight):
    for tiles, pos, weight in ((src, src_pos, src_weight), (tgt, tgt_pos, tgt_weight)):
        for q in range(2 * OWN):
            pos[:, q * LANES : q * LANES + LANES] = tiles[q * 4 : q * 4 + 3, :]
        weight[...] = tiles[pl.ds(3, 2 * OWN, stride=4), :]


def shards(
    dims,
    src_pos,
    src_weight,
    src_pot,
    src_count,
    tgt_pos,
    tgt_weight,
    tgt_pot,
    tgt_count,
    requests,
    pair_src,
    pair_slot,
    pair_count,
):
    nx, nz, ny, nc = dims
    n_tgt, n_clus = ny * nc, nx * nz
    slots = n_clus * REQ
    pairs = pair_src.shape[0]
    quarters = 2 * OWN

    def tall(v):
        return v.reshape(*v.shape[:-1], quarters, LANES)

    vmem = pl.BlockSpec(memory_space=pltpu.VMEM)
    dma = pltpu.SemaphoreType.DMA
    inputs = [
        tgt_pos,
        tall(tgt_weight),
        tall(tgt_pot),
        tgt_count,
        requests.T,
        src_pos,
        tall(src_weight),
        tall(src_pot),
        src_count,
        pair_count[None, :],
        pair_src[None, :],
        pair_slot[None, :],
    ]
    spaces = [pltpu.SMEM if i in (3, 4, 8) else pltpu.VMEM for i in range(12)]
    tiles = jax.ShapeDtypeStruct((8 * OWN, LANES), f32)
    sums = pl.pallas_call(
        functools.partial(kernel, dims),
        out_shape=[tiles, tiles],
        in_specs=[[pl.BlockSpec(memory_space=pltpu.HBM)] * len(inputs)],
        out_specs=[vmem] * 2,
        scratch_shapes=[
            [space(v.shape, v.dtype) for space, v in zip(spaces, inputs)],
            dma((len(inputs),)),
            pltpu.VMEM((1, pairs), jnp.int32),
            pltpu.VMEM((1, pairs), jnp.int32),
            pltpu.SMEM((1, pairs), jnp.int32),
            pltpu.SMEM((1, pairs), jnp.int32),
            dma((2,)),
            pltpu.VMEM((n_tgt, 8 * OWN, LANES), f32),
            pltpu.VMEM((nx, 8 * OWN, LANES), f32),
            pltpu.VMEM((nz, nx, REQ, 8, LANES), f32),
            pltpu.VMEM((nz, nx, REQ, 8, LANES), f32),
            pltpu.VMEM((nz, nx, REQ, LANES), jnp.int32),
            pltpu.VMEM((nz, nx, REQ, LANES), jnp.int32),
            pltpu.VMEM((n_clus, REQ, LANES), jnp.int32),
            pltpu.VMEM((n_tgt * OWN, 48, BLK), bf16),
            pltpu.VMEM((slots, 48, BLK), bf16),
            pltpu.VMEM((n_tgt * OWN, 16, BLK), bf16),
            pltpu.VMEM((slots, 16, BLK), bf16),
            pltpu.VMEM((n_tgt * OWN, 32, BLK), f8),
            pltpu.VMEM((slots, 32, BLK), f8),
            pltpu.VMEM((pairs * 8, LANES), f32),
            pltpu.VMEM((pairs * 8, LANES), f32),
            pltpu.VMEM((n_tgt * OWN * 8, LANES), f32),
            pltpu.VMEM((slots * 8, LANES), f32),
            pltpu.VMEM((n_tgt, 8 * OWN, LANES), f32),
            pltpu.VMEM((n_clus, 8 * REQ, LANES), f32),
            pltpu.VMEM((8 * OWN, LANES), f32),
            dma((nx,)),
            dma((nx,)),
            dma((nz,)),
            dma((nz,)),
            dma((ny, nc)),
            dma((ny, nc)),
            dma((nz, nx)),
            dma((nz, nx)),
            dma((nx, nz)),
            dma((nx, nz)),
            dma((nx, nz)),
            dma((nx, nz)),
            dma((ny, nc)),
            dma((ny, nc)),
        ],
        compiler_params=pltpu.CompilerParams(
            collective_id=0, has_side_effects=True, vmem_limit_bytes=48 << 20
        ),
    )(
        [
            v if v.size == 1 else pltpu.with_memory_space_constraint(v, pltpu.HBM)
            for v in inputs
        ]
    )
    pos = jax.ShapeDtypeStruct((3, quarters * LANES), f32)
    weight = jax.ShapeDtypeStruct((quarters, LANES), f32)
    outs = pl.pallas_call(
        write_out,
        out_shape=[pos, weight, pos, weight],
        in_specs=[vmem] * 2,
        compiler_params=pltpu.CompilerParams(vmem_limit_bytes=4 << 20),
    )(*sums)
    return outs[0], outs[1].reshape(-1), outs[2], outs[3].reshape(-1)


def solution(mesh):
    n_clus, n_tgt = mesh.shape["clus"], mesh.shape["tgt"]
    nx = math.isqrt(n_clus)
    dims = (nx, n_clus // nx, n_tgt // 2, 2)
    torus = Mesh(mesh.devices.reshape(dims), AXES)
    wide, flat = P(None, AXES), P(AXES)
    return jax.shard_map(
        functools.partial(shards, dims),
        mesh=torus,
        in_specs=(
            wide,
            flat,
            flat,
            flat,
            wide,
            flat,
            flat,
            flat,
            P(AXES, None),
            flat,
            flat,
            flat,
        ),
        out_specs=(wide, flat, wide, flat),
        check_vma=False,
    )
```
